128 devices in a mesh: cells: 128 (over x, z, y, core).
Axes of the slice: x: 4, y: 4, z: 4, core: 2. Of those that a mesh axis runs over, the one named last changes fastest.
Arguments:
- parcel_locations: float32 [3, 655360], P(None, 'cells'), may hold values from 0 to 1.2
- parcel_speed: float32 [3, 655360], P(None, 'cells'), may hold values from -6 to 6
- explicit_forcing: float32 [3, 655360], P(None, 'cells'), may hold values from -6 to 6
- parcel_weight: float32 [655360], P('cells'), may hold values from 0.5 to 2
- scaled_heat: float32 [655360], P('cells'), may hold values from 0 to 1
- solid_share: float32 [655360], P('cells'), may hold values from 0 to 0.4
- alive_tally: int32 [10240], P('cells'), may hold values from 1 to 64, as said below
- target_processor: int32 [10240], P('cells'), may hold values from 0 to 127, as said below
- target_place: int32 [10240], P('cells'), may hold values from 0 to 79, as said below
- adjacent_bins: int32 [27, 10240], P(None, 'cells'), may hold values from 0 to 10239, as said below
Outputs:
- new_velocity: float32 [3, 655360], P(None, 'cells')
- density: float32 [655360], P('cells')
The draws below stay inside these ranges and needn't reach their ends.
Inputs may be any that keep to these rules, and one draw needn't show every extreme that they name: `target_processor`: one device's blocks go to exactly 40 distinct devices, exactly 2 blocks to each; every device receives exactly 80 blocks. The pairs (target_processor, target_place) of all blocks are distinct, so every slot of every device receives one block. `adjacent_bins`: entry 13 of a cell is the cell itself. Every other entry of a cell on device d names a different cell on device d, one of the last 40 cells of device d - 1, or one of the first 40 cells of device d + 1 (global index = device * 80 + slot). Entries may repeat. `alive_tally`: 64 is reached.
All inputs are finite; a program needn't handle non-finite values.
Results may differ from the reference program's by a relative error of at most 0.00013.
Values sent between devices are 32-bit elements; how exact they have to be, the bound alone decides.
No kernel may reach another device: no remote copies, remote signals or barrier semaphores. Data moves between devices by JAX's collectives and lax.ppermute only.
A program may use at most 64 MiB of HBM per device.

```python
import jax
import jax.numpy as jnp
from jax import lax

BIN_PLACES = 64
NEIGH = 27
CELLS_DEV = 80
NODES = 128
CAP = 2
RIM = 40
TOTAL_CELLS = 10240
BODY_PLACES = 655360


def shuffle_rows(key_rows):

    def one_row(sub_key):
        return jax.random.permutation(sub_key, CELLS_DEV)
    return jax.vmap(one_row)(key_rows)


def migration_plan(key):
    group_count = CELLS_DEV // CAP
    key_rank, key_spread, key_offset, key_order, key_slot = jax.random.split(jax.random.fold_in(key, 31), 5)
    ranking = jax.random.permutation(key_rank, NODES)
    spread = jax.random.permutation(key_spread, NODES)
    offsets = jax.random.permutation(key_offset, NODES)[:group_count]
    target_peer = spread[(ranking[:, None] + offsets[None, :]) % NODES]
    orders = shuffle_rows(jax.random.split(key_order, NODES))
    slot_perm = shuffle_rows(jax.random.split(key_slot, NODES))
    position = jnp.arange(CELLS_DEV)
    peer_by_pos = target_peer[:, position // CAP]
    slot_by_pos = slot_perm[peer_by_pos, position[None, :]]
    source_rows = jnp.arange(NODES)[:, None]
    device_table = jnp.zeros((NODES, CELLS_DEV), jnp.int32).at[source_rows, orders].set(peer_by_pos.astype(jnp.int32))
    slot_table = jnp.zeros((NODES, CELLS_DEV), jnp.int32).at[source_rows, orders].set(slot_by_pos.astype(jnp.int32))
    return (device_table.reshape(-1).astype(jnp.int32), slot_table.reshape(-1).astype(jnp.int32))


def draw_target_processor(key, part):
    return migration_plan(key)[0]


def draw_target_place(key, part):
    return migration_plan(key)[1]


def draw_alive_tally(key, part):
    key_full, key_rest = jax.random.split(jax.random.fold_in(key, 5), 2)
    full_cells = jax.random.randint(key_full, (TOTAL_CELLS,), 0, 4) == 0
    partial_value = jax.random.randint(key_rest, (TOTAL_CELLS,), 1, BIN_PLACES)
    alive_tally = jnp.where(full_cells, BIN_PLACES, partial_value).astype(jnp.int32)
    return alive_tally.at[0].set(BIN_PLACES)


def draw_adjacent_bins(key, part):
    extent = CELLS_DEV + 2 * RIM
    global_cell = jnp.arange(TOTAL_CELLS)
    device_of = global_cell // CELLS_DEV
    local_of = global_cell % CELLS_DEV
    picks = jax.random.randint(jax.random.fold_in(key, 11), (NEIGH - 1, TOTAL_CELLS), 0, extent - 1)
    own_place = local_of + RIM
    picks = picks + (picks >= own_place[None, :]).astype(picks.dtype)
    left_bad = (device_of[None, :] == 0) & (picks < RIM)
    right_bad = (device_of[None, :] == NODES - 1) & (picks >= CELLS_DEV + RIM)
    repaired = RIM + (local_of[None, :] + 1 + picks % (CELLS_DEV - 1)) % CELLS_DEV
    picks = jnp.where(left_bad | right_bad, repaired, picks)
    chosen = picks - RIM + device_of[None, :] * CELLS_DEV
    table = jnp.concatenate([chosen[:13], global_cell[None, :], chosen[13:]], 0)
    return table.astype(jnp.int32)


def block_scale(stream_key, shape, pieces, smallest, largest):
    def one(dim, blocks):
        steps = jax.random.uniform(jax.random.fold_in(jax.random.fold_in(stream_key, 6), dim), (blocks,), jnp.float32, smallest / len(pieces), largest / len(pieces))
        return jnp.repeat(jnp.exp(steps), shape[dim] // blocks).reshape((-1,) + (1,) * (len(shape) - dim - 1))

    gain = one(*pieces[0])
    for cut in pieces[1:]:
        gain = gain * one(*cut)
    return gain


def normal_values(stream_key, shape, scale, bound, cuts=(), held_as=jnp.bfloat16):
    entries = jax.random.normal(stream_key, shape, jnp.float32) * scale
    if len(cuts) > 0:
        entries = block_scale(stream_key, shape, cuts, -0.22, 0.18) * entries
    return jnp.clip(entries, min=-bound, max=bound).astype(held_as)


def setup_inputs(seed: int = 0) -> dict:
    splits = jax.random.split(jax.random.key(seed), 11)
    return {
        "parcel_locations": jnp.clip(1.2 * jax.random.uniform(splits[0], (3, BODY_PLACES), jnp.float32) ** block_scale(splits[0], (3, BODY_PLACES), ((1, 128),), -0.2, 0.2), 0.0, 1.2),
        "parcel_speed": normal_values(splits[1], (3, BODY_PLACES), 1.0, 6.0, ((1, 128),), jnp.float32),
        "explicit_forcing": normal_values(splits[2], (3, BODY_PLACES), 1.0, 6.0, ((1, 128),), jnp.float32),
        "parcel_weight": jnp.clip(0.5 + 1.5 * jax.random.uniform(splits[3], (BODY_PLACES,), jnp.float32) ** block_scale(splits[3], (BODY_PLACES,), ((0, 128),), -0.2, 0.2), 0.5, 2.0),
        "scaled_heat": jnp.clip(1.0 * jax.random.uniform(splits[4], (BODY_PLACES,), jnp.float32) ** block_scale(splits[4], (BODY_PLACES,), ((0, 128),), -0.2, 0.2), 0.0, 1.0),
        "solid_share": jnp.clip(0.4 * jax.random.uniform(splits[5], (BODY_PLACES,), jnp.float32) ** block_scale(splits[5], (BODY_PLACES,), ((0, 128),), -0.2, 0.2), 0.0, 0.4),
        "alive_tally": draw_alive_tally(jax.random.fold_in(splits[10], 71), 0),
        "target_processor": draw_target_processor(jax.random.fold_in(splits[10], 71), 0),
        "target_place": draw_target_place(jax.random.fold_in(splits[10], 71), 0),
        "adjacent_bins": draw_adjacent_bins(jax.random.fold_in(splits[10], 71), 0),
    }


step_time = 0.5
mass_rate = 0.3
visc_scale = 0.01
dens_scale = 0.01
heat_slope = 3.0
jamming_bound = 0.6
centre_entry = 13


def stiffness_of_heat(scaled_heat, solid_share):
    return jnp.exp(-heat_slope * scaled_heat) * (1.0 - solid_share / jamming_bound) ** (-2.5)


def base_weights(own_pos, other_pos):
    dist_sq = (own_pos[:, 0, :, None] - other_pos[:, 0, None, :]) ** 2
    dist_sq = dist_sq + (own_pos[:, 1, :, None] - other_pos[:, 1, None, :]) ** 2
    dist_sq = dist_sq + (own_pos[:, 2, :, None] - other_pos[:, 2, None, :]) ** 2
    return jnp.maximum(1.0 - dist_sq, 0.0)


def density_turn(own_pos, source_pos, source_mass):
    def advance(entry_index, index_row, carried):
        other_pos = jnp.take(source_pos, index_row, axis=0)
        other_mass = jnp.take(source_mass, index_row, axis=0)
        weight = base_weights(own_pos, other_pos)
        return carried + jnp.sum(weight * weight * weight * other_mass[:, None, :], axis=2)
    return advance


def viscous_turn(own_pos, own_visc, source_pos, source_visc, source_coef, source_vel):
    off_diagonal = 1.0 - jnp.eye(BIN_PLACES, dtype=jnp.float32)

    def advance(entry_index, index_row, carried):
        numer, denom = carried
        other_pos = jnp.take(source_pos, index_row, axis=0)
        other_visc = jnp.take(source_visc, index_row, axis=0)
        other_coef = jnp.take(source_coef, index_row, axis=0)
        other_vel = jnp.take(source_vel, index_row, axis=0)
        weight = base_weights(own_pos, other_pos)
        mean_visc = 2.0 * own_visc[:, :, None] * other_visc[:, None, :] / (own_visc[:, :, None] + other_visc[:, None, :])
        couple = mean_visc * weight * weight * other_coef[:, None, :]
        couple = jnp.where(entry_index == centre_entry, couple * off_diagonal, couple)
        numer = numer + jnp.einsum("bij,bcj->bci", couple, other_vel, precision=lax.Precision.HIGHEST)
        denom = denom + jnp.sum(couple, axis=2)
        return numer, denom
    return advance


def finish(numer, denom, rate_mass, own_vstar, live):
    total_diag = rate_mass + denom
    safe_diag = jnp.where(live > 0, total_diag, 1.0)
    value = (rate_mass[:, None, :] * own_vstar + numer) / safe_diag[:, None, :]
    return jnp.where(live[:, None, :] > 0, value, 0.0)


def reference(parcel_locations, parcel_speed, explicit_forcing, parcel_weight, scaled_heat, solid_share, alive_tally, target_processor, target_place, adjacent_bins):
    whole_bin_total = alive_tally.shape[0]
    slot_iota = lax.broadcasted_iota(jnp.int32, (whole_bin_total, BIN_PLACES), 1)
    live_before = (slot_iota < alive_tally[:, None]).astype(jnp.float32)
    trial_speed_vector = parcel_speed + step_time * explicit_forcing
    hidden_entries = parcel_weight.reshape(whole_bin_total, BIN_PLACES) * live_before
    quantity_stack = jnp.concatenate([parcel_locations.reshape(3, whole_bin_total, BIN_PLACES), trial_speed_vector.reshape(3, whole_bin_total, BIN_PLACES), hidden_entries[None], scaled_heat.reshape(1, whole_bin_total, BIN_PLACES), solid_share.reshape(1, whole_bin_total, BIN_PLACES)], 0)
    quantity_stack = jnp.transpose(quantity_stack, (1, 0, 2))
    target = (target_processor * CELLS_DEV + target_place).astype(jnp.int32)
    relocated = jnp.zeros_like(quantity_stack).at[target].set(quantity_stack)
    moved_count = jnp.zeros_like(alive_tally).at[target].set(alive_tally)
    live = (slot_iota < moved_count[:, None]).astype(jnp.float32)
    all_pos = relocated[:, 0:3]
    all_vstar = relocated[:, 3:6]
    all_mass = relocated[:, 6]
    whole_stiffness = stiffness_of_heat(relocated[:, 7], relocated[:, 8])
    block_count = whole_bin_total // CELLS_DEV
    index_blocks = jnp.transpose(adjacent_bins.reshape(NEIGH, block_count, CELLS_DEV), (1, 0, 2))

    def by_block(values):
        return values.reshape((block_count, CELLS_DEV) + values.shape[1:])

    def density_block(packed):
        own_pos, index_rows = packed
        advance = density_turn(own_pos, all_pos, all_mass)

        def loop_body(entry_index, carried):
            return advance(entry_index, index_rows[entry_index], carried)
        return lax.fori_loop(0, NEIGH, loop_body, jnp.zeros((CELLS_DEV, BIN_PLACES), jnp.float32))

    raw = dens_scale * lax.map(density_block, (by_block(all_pos), index_blocks)).reshape(whole_bin_total, BIN_PLACES)
    safe = jnp.where(live > 0, raw, 1.0)
    density = jnp.where(live > 0, raw, 0.0)
    all_coef = visc_scale * all_mass / safe
    rate_mass = mass_rate * all_mass

    def sweep(old_vel):
        def sweep_block(packed):
            own_pos, own_visc, index_rows = packed
            advance = viscous_turn(own_pos, own_visc, all_pos, whole_stiffness, all_coef, old_vel)

            def loop_body(entry_index, carried):
                return advance(entry_index, index_rows[entry_index], carried)
            start = (jnp.zeros((CELLS_DEV, 3, BIN_PLACES), jnp.float32), jnp.zeros((CELLS_DEV, BIN_PLACES), jnp.float32))
            return lax.fori_loop(0, NEIGH, loop_body, start)
        numer, denom = lax.map(sweep_block, (by_block(all_pos), by_block(whole_stiffness), index_blocks))
        return finish(numer.reshape(whole_bin_total, 3, BIN_PLACES), denom.reshape(whole_bin_total, BIN_PLACES), rate_mass, all_vstar, live)

    first_sweep = sweep(all_vstar)
    second_sweep = sweep(first_sweep)
    new_velocity = jnp.transpose(second_sweep, (1, 0, 2)).reshape(3, whole_bin_total * BIN_PLACES)
    return new_velocity, density.reshape(whole_bin_total * BIN_PLACES)
```

```python
import functools

import jax
import jax.numpy as jnp
from jax import lax
from jax.experimental import pallas as pl
from jax.experimental.pallas import tpu as pltpu
from jax.sharding import PartitionSpec as P

SLOTS = 64
NEIGH = 27
ENTRY_ORDER = (13,) + tuple(range(13)) + tuple(range(14, 27))
ROWS = 14
WIDTH = ROWS * 128
CHUNK = 32
GROUP = 8
FIELDS = 8
PEER_ROWS = FIELDS + 1
TERMS = 32

step_time = 0.5
mass_rate = 0.3
visc_scale = 0.01
dens_scale = 0.01
heat_slope = 3.0
jamming_bound = 0.6

VMEM = pltpu.MemorySpace.VMEM
SMEM = pltpu.MemorySpace.SMEM
HBM = pltpu.MemorySpace.HBM
MIB = 1 << 20
BF16 = jnp.bfloat16
F32 = jnp.float32


def lane_iota(shape):
    return lax.broadcasted_iota(jnp.int32, shape, len(shape) - 1)


def sub_iota(shape):
    return lax.broadcasted_iota(jnp.int32, shape, len(shape) - 2)


def split_bf16(value, count):
    parts = []
    for _ in range(count):
        part = value.astype(BF16).astype(F32)
        parts.append(part)
        value = value - part
    return parts


def pack_kernel(*refs):
    inputs, sent, local, out, fields, seen, sems, out_sem = refs[:9], refs[9], refs[10:19], *refs[19:]
    copies = [pltpu.make_async_copy(a, b, sems.at[i]) for i, (a, b) in enumerate(zip(inputs, local))]
    for copy in copies:
        copy.start()
    tally, peer, place, pos, speed, force, weight, heat, share = local
    cells = tally.shape[0]
    peers = out.shape[0] // PEER_ROWS
    lane = lane_iota((1, 128))
    low = lane < SLOTS

    def clear(index, carry):
        seen[index] = 0
        out[pl.ds(index * PEER_ROWS + FIELDS, 1), :] = jnp.full((1, 128), -1.0, F32)
        return carry

    lax.fori_loop(0, peers, clear, 0, unroll=8)
    for copy in copies:
        copy.wait()
    open_bound = 1.0 - share[...] / jamming_bound
    resist = jnp.exp(heat_slope * heat[...]) * (open_bound * open_bound * jnp.sqrt(open_bound))
    for pair in range(cells // 2):
        span = pl.ds(pair * 128, 128)
        bound = jnp.where(low, tally[2 * pair], tally[2 * pair + 1] + SLOTS)
        live = (lane < bound).astype(F32)
        fields[pair, 0:3, :] = pos[:, span]
        fields[pair, 3:6, :] = speed[:, span] + step_time * force[:, span]
        fields[pair, 6:7, :] = weight[pair : pair + 1, :] * live
        fields[pair, 7:8, :] = resist[pair : pair + 1, :]
    half_of = lane_iota((FIELDS, 128)) // SLOTS

    def send(pair, carry):
        tile = fields[pair]
        turned = pltpu.roll(tile, SLOTS, 1)
        for side in range(2):
            cell = 2 * pair + side
            target = peer[cell]
            half = seen[target]
            seen[target] = 1
            row = target * PEER_ROWS
            value = jnp.where(half == side, tile, turned)
            pltpu.store(out.at[pl.ds(row, FIELDS), :], value, mask=half_of == half)
            first = half * SLOTS
            head = jnp.where(lane == first, place[cell].astype(F32), tally[cell].astype(F32))
            pltpu.store(
                out.at[pl.ds(row + FIELDS, 1), :], head, mask=(lane == first) | (lane == first + 1)
            )
        return carry

    lax.fori_loop(0, cells // 2, send, 0, unroll=4)
    copy = pltpu.make_async_copy(out, sent, out_sem)
    copy.start()
    copy.wait()


def unpack_kernel(got, head, tail, count, heads_v, heads_s, store, sem):
    peers = got.shape[0] // PEER_ROWS
    pairs = store.shape[0] - 1
    heads = jnp.transpose(got[pl.ds(FIELDS, peers, stride=PEER_ROWS), :])
    heads_v[0:2, :] = heads[0:2].astype(jnp.int32)
    heads_v[2:4, :] = heads[SLOTS : SLOTS + 2].astype(jnp.int32)
    copy = pltpu.make_async_copy(heads_v, heads_s, sem)
    copy.start()
    copy.wait()
    half_of = lane_iota((FIELDS, 128)) // SLOTS

    def take(source, carry):
        tile = got[pl.ds(source * PEER_ROWS, FIELDS), :]
        turned = pltpu.roll(tile, SLOTS, 1)
        for half in range(2):
            slot = heads_s[2 * half, source]
            slot = jnp.where(slot < 0, 2 * pairs, slot)
            count[slot] = heads_s[2 * half + 1, source]
            side = lax.rem(slot, 2)
            value = jnp.where(side == half, tile, turned)
            pltpu.store(store.at[slot // 2], value, mask=half_of == side)
        return carry

    lax.fori_loop(0, peers, take, 0, unroll=8)
    head[...] = store[0 : pairs // 2]
    tail[...] = store[pairs // 2 : pairs]


def two_halves(tile, low):
    turned = pltpu.roll(tile, SLOTS, 1)
    return (tile, turned), low


def put_halves(tile, low, first, second, index):
    turned = pltpu.roll(tile, SLOTS, 1)
    zero = jnp.zeros_like(tile)
    first[index] = jnp.where(low, tile, zero).astype(first.dtype)
    second[index] = jnp.where(low, zero, turned).astype(first.dtype)
    first[index + 1] = jnp.where(low, turned, zero).astype(first.dtype)
    second[index + 1] = jnp.where(low, zero, tile).astype(first.dtype)


def entries(adj, base, cell, dummy):
    return [adj[n, cell] - base for n in ENTRY_ORDER] + [dummy]


def density_kernel(
    base_ref, adj, count, left, head, tail, right, hi, lo, dens, coef_head, coef_tail,
    terms_a, terms_b, ext, stage, lhs, own_r, rows_t, rows_f, acc, raw,
):
    rim = 2 * head.shape[0]
    quarter = head.shape[0]
    dummy = 4 * rim
    base = base_ref[0]
    step = pl.program_id(0)
    low8 = lane_iota((FIELDS, 128)) < SLOTS
    low32 = lane_iota((TERMS, 128)) < SLOTS
    sub8 = sub_iota((FIELDS, 128))

    @pl.when(step == 0)
    def _():
        ext[dummy] = jnp.where(sub8 == 7, 1.0, 0.0)
        terms_a[dummy] = jnp.zeros((TERMS, 128), BF16)
        terms_b[dummy] = jnp.zeros((TERMS, 128), BF16)
        ones = jnp.where(sub8 < 3, 1.0, 0.0)
        for part, ref in enumerate((left, head, tail, right)):
            for pair in range(quarter):
                tile = ref[pair]
                slot = part * rim + 2 * pair
                turned = pltpu.roll(tile, SLOTS, 1)
                ext[slot] = jnp.where(low8, tile, turned)
                ext[slot + 1] = jnp.where(low8, turned, tile)
                x, y, z = tile[0:1], tile[1:2], tile[2:3]
                length = x * x + y * y + z * z
                vector = jnp.where(sub8 == 3, -length, tile)
                v1, v2, v3 = split_bf16(vector, 3)
                at = slot // 2 % 8
                for row, v in enumerate((v1, v2, v3, v1, v2, v1)):
                    stage[at, 4 * row : 4 * row + 4, :] = v[0:4]
                stage[at, 24:32, :] = ones
                put_halves(stage[at], low32, terms_a, terms_b, slot)
                if part in (1, 2):
                    own = (part - 1) * quarter + pair
                    vector = jnp.where(sub8 == 3, 1.0, 2.0 * tile)
                    w1, w2, w3 = split_bf16(vector, 3)
                    a1, a2, a3 = split_bf16(1.0 - length, 3)
                    at = 8 + pair % 8
                    for row, w in enumerate((w1, w1, w1, w2, w2, w3)):
                        stage[at, 4 * row : 4 * row + 4, :] = w[0:4]
                    extra = jnp.where(sub8 == 0, a1, jnp.where(sub8 == 1, a2, a3))
                    stage[at, 24:32, :] = jnp.where(sub8 < 3, extra, tile[7:8])
                    turned = jnp.transpose(stage[at])
                    lhs[own] = turned.astype(BF16)
                    own_r[own] = jnp.broadcast_to(turned[:, 31:32], (128, 128))

    chunk_lane = lane_iota((CHUNK, 128))
    chunk_sub = sub_iota((CHUNK, 128))

    def one_cell(local, carry):
        cell = step * GROUP + local
        index = entries(adj, base, cell, dummy)
        for p in range(ROWS):
            i, j = index[2 * p], index[2 * p + 1]
            rows_f[p] = jnp.where(low8, ext[i], ext[j])
            rows_t[:, p * 128 : p * 128 + 128] = terms_a[i] + terms_b[j]

        def turn(part, carry):
            first = pl.multiple_of(part * CHUNK, CHUNK)
            place = pl.multiple_of(lax.rem(cell, 2) * SLOTS + first, CHUNK)
            own = lhs[cell // 2, pl.ds(place, CHUNK), :]
            ri = own_r[cell // 2, pl.ds(place, CHUNK), :]
            total = jnp.zeros((CHUNK, 128), F32)
            for p2 in range(ROWS // 2):
                wide = jnp.dot(
                    own, rows_t[:, p2 * 256 : p2 * 256 + 256], preferred_element_type=F32
                )
                for p in (2 * p2, 2 * p2 + 1):
                    q = jnp.maximum(wide[:, (p % 2) * 128 : (p % 2) * 128 + 128], 0.0)
                    q2 = q * q
                    total = total + q2 * (q * rows_f[p, 6:7, :])
                    value = q2 * pl.reciprocal(ri + rows_f[p, 7:8, :])
                    if p == 0:
                        value = jnp.where(chunk_lane == chunk_sub + first, 0.0, value)
                    upper = value.astype(BF16)
                    span = slice(p * 128, p * 128 + 128)
                    hi[local, pl.ds(first, CHUNK), span] = upper
                    lo[local, pl.ds(first, CHUNK), span] = (value - upper.astype(F32)).astype(BF16)
            acc[cell, pl.ds(first, CHUNK), :] = total
            return carry

        return lax.fori_loop(0, (count[cell] + CHUNK - 1) // CHUNK, turn, carry)

    lax.fori_loop(0, GROUP, one_cell, 0)

    @pl.when(step == pl.num_programs(0) - 1)
    def _():
        ones = jnp.ones((FIELDS, 128), BF16)

        def reduce_pair(pair, carry):
            total = jnp.zeros((FIELDS, 128), F32)
            for part in split_bf16(acc[pl.ds(2 * pair, 2)].reshape(2 * SLOTS, 128), 3):
                total = total + lax.dot_general(
                    ones, part.astype(BF16), (((1,), (1,)), ((), ())), preferred_element_type=F32
                )
            raw[pl.ds(pair, 1), :] = total[0:1]
            return carry

        lax.fori_loop(0, 2 * quarter, reduce_pair, 0, unroll=4)
        for part, (ref, coef) in enumerate(((head, coef_head), (tail, coef_tail))):
            mass = ref[:, 6, :]
            live = mass > 0.0
            value = dens_scale * raw[part * quarter : (part + 1) * quarter, :]
            dens[part * quarter : (part + 1) * quarter, :] = jnp.where(live, value, 0.0)
            coef[...] = (2.0 * visc_scale) * mass / jnp.where(live, value, 1.0)


def sweep_kernel(is_first, base_ref, adj, hi, lo, *refs):
    coefs, speeds, refs = refs[:4], refs[4:8], refs[8:]
    if is_first:
        (head, tail), (out_head, out_tail), refs = speeds[1:3], refs[:2], refs[2:]
    else:
        (head, tail), (out,), refs = refs[:2], refs[2:3], refs[3:]
    ext_a, ext_b, rows, sums, stage = refs
    quarter = head.shape[0]
    rim = 2 * quarter
    dummy = 4 * rim
    base = base_ref[0]
    step = pl.program_id(0)
    low = lane_iota((FIELDS, 128)) < SLOTS
    low16 = lane_iota((2 * FIELDS, 128)) < SLOTS
    sub = sub_iota((FIELDS, 128))
    moving = (sub >= 3) & (sub < 6)

    @pl.when(step == 0)
    def _():
        ext_a[dummy] = jnp.zeros((2 * FIELDS, 128), BF16)
        ext_b[dummy] = jnp.zeros((2 * FIELDS, 128), BF16)
        for part in range(4):
            for pair in range(quarter):
                tile = jnp.where(sub == 0, 1.0, jnp.where(moving, speeds[part][pair], 0.0))
                w1, w2 = split_bf16(tile * coefs[part][pair : pair + 1, :], 2)
                at = pair % 8
                stage[at, 0:FIELDS, :] = w1
                stage[at, FIELDS:, :] = w2
                put_halves(stage[at], low16, ext_a, ext_b, part * rim + 2 * pair)

    def one_cell(local, carry):
        cell = step * GROUP + local
        index = entries(adj, base, cell, dummy)
        at = lax.rem(local, 4)
        for p in range(ROWS):
            rows[at, :, p * 128 : p * 128 + 128] = ext_a[index[2 * p]] + ext_b[index[2 * p + 1]]
        total = jnp.zeros((2 * FIELDS, SLOTS), F32)
        for part in (hi, lo):
            total = total + lax.dot_general(
                rows[at], part[local], (((1,), (1,)), ((), ())), preferred_element_type=F32
            )
        sums[cell, :, 0:SLOTS] = total[0:FIELDS] + total[FIELDS:]
        return carry

    lax.fori_loop(0, GROUP, one_cell, 0, unroll=4)

    @pl.when(step == pl.num_programs(0) - 1)
    def _():
        for part, ref in enumerate((head, tail)):
            for pair in range(quarter):
                slot = part * quarter + pair
                tile = ref[pair]
                total = jnp.where(low, sums[2 * slot], pltpu.roll(sums[2 * slot + 1], SLOTS, 1))
                live = jnp.broadcast_to(tile[6:7] > 0.0, (FIELDS, 128))
                rate = mass_rate * tile[6:7]
                below = jnp.broadcast_to(rate + total[0:1], (FIELDS, 128))
                value = (rate * tile + total) / jnp.where(live, below, 1.0)
                value = jnp.where(live & moving, value, 0.0)
                if is_first:
                    (out_head, out_tail)[part][pair] = value
                else:
                    out[:, slot * 128 : slot * 128 + 128] = value[3:6]


def call(kernel, outs, scratch, in_specs, args, out_specs=None, grid=None, vmem=40):
    extra = {} if grid is None else {"grid": grid}
    return pl.pallas_call(
        kernel,
        out_shape=outs,
        in_specs=in_specs,
        out_specs=out_specs,
        scratch_shapes=scratch,
        compiler_params=pltpu.CompilerParams(vmem_limit_bytes=vmem * MIB),
        **extra,
    )(*args)


def f32(*shape):
    return jax.ShapeDtypeStruct(shape, F32)


def spec(space):
    return pl.BlockSpec(memory_space=space)


def whole(*shape):
    return pl.BlockSpec(shape, lambda g: (0,) * len(shape))


def density(base, adj, count, left, head, tail, right):
    quarter = head.shape[0]
    cells, pairs = 4 * quarter, 2 * quarter
    ext = 2 * cells + 1
    tile = whole(quarter, FIELDS, 128)
    block = pl.BlockSpec((GROUP, SLOTS, WIDTH), lambda g: (g, 0, 0))
    return call(
        density_kernel,
        [jax.ShapeDtypeStruct((cells, SLOTS, WIDTH), BF16)] * 2
        + [f32(pairs, 128), f32(quarter, 128), f32(quarter, 128)],
        [pltpu.VMEM((ext, TERMS, 128), BF16)] * 2
        + [
            pltpu.VMEM((ext, FIELDS, 128), F32),
            pltpu.VMEM((16, TERMS, 128), F32),
            pltpu.VMEM((pairs, 128, TERMS), BF16),
            pltpu.VMEM((pairs, 128, 128), F32),
            pltpu.VMEM((TERMS, WIDTH), BF16),
            pltpu.VMEM((ROWS, FIELDS, 128), F32),
            pltpu.VMEM((cells, SLOTS, 128), F32),
            pltpu.VMEM((pairs, 128), F32),
        ],
        [spec(SMEM)] * 3 + [tile] * 4,
        (base, adj, count, left, head, tail, right),
        out_specs=[block] * 2 + [whole(pairs, 128), whole(quarter, 128), whole(quarter, 128)],
        grid=(cells // GROUP,),
    )


def sweep(is_first, base, adj, hi, lo, coefs, speeds, head, tail):
    quarter = head.shape[0]
    cells = 4 * quarter
    ext = 2 * cells + 1
    tile = whole(quarter, FIELDS, 128)
    block = pl.BlockSpec((GROUP, SLOTS, WIDTH), lambda g: (g, 0, 0))
    own = () if is_first else (head, tail)
    if is_first:
        outs, out_specs = [f32(quarter, FIELDS, 128)] * 2, [tile] * 2
    else:
        outs, out_specs = [f32(3, cells * SLOTS)], [whole(3, cells * SLOTS)]
    return call(
        functools.partial(sweep_kernel, is_first),
        outs,
        [pltpu.VMEM((ext, 2 * FIELDS, 128), BF16)] * 2
        + [
            pltpu.VMEM((4, 2 * FIELDS, WIDTH), BF16),
            pltpu.VMEM((cells, FIELDS, 128), F32),
            pltpu.VMEM((8, 2 * FIELDS, 128), F32),
        ],
        [spec(SMEM)] * 2 + [block] * 2 + [whole(quarter, 128)] * 4 + [tile] * (4 + len(own)),
        (base, adj, hi, lo) + tuple(coefs) + tuple(speeds) + own,
        out_specs=out_specs,
        grid=(cells // GROUP,),
    )


def body(pos, speed, force, weight, heat, share, tally, peer, place, adj):
    peers = lax.axis_size("cells")
    rank = lax.axis_index("cells")
    cells = tally.shape[0]
    rim = cells // 2
    quarter = cells // 4
    pairs = cells // 2
    right_going = [(i, i + 1) for i in range(peers - 1)]
    left_going = [(i + 1, i) for i in range(peers - 1)]

    def rims(head, tail):
        return lax.ppermute(tail, "cells", right_going), lax.ppermute(head, "cells", left_going)

    args = (tally, peer, place, pos, speed, force)
    args = args + tuple(v.reshape(pairs, 128) for v in (weight, heat, share))
    (sent,) = call(
        pack_kernel,
        [pltpu.HBM((peers * PEER_ROWS, 128), F32)],
        [(pltpu.SMEM if i < 3 else pltpu.VMEM)(v.shape, v.dtype) for i, v in enumerate(args)]
        + [
            pltpu.VMEM((peers * PEER_ROWS, 128), F32),
            pltpu.VMEM((pairs, FIELDS, 128), F32),
            pltpu.SMEM((peers,), jnp.int32),
            pltpu.SemaphoreType.DMA((9,)),
            pltpu.SemaphoreType.DMA,
        ],
        [spec(pl.ANY)] * 9,
        args,
        out_specs=[spec(HBM)],
    )
    got = lax.all_to_all(
        sent.reshape(peers, 1, PEER_ROWS * 128), "cells", split_axis=0, concat_axis=0, tiled=True
    )
    head, tail, count = call(
        unpack_kernel,
        [f32(quarter, FIELDS, 128)] * 2 + [jax.ShapeDtypeStruct((cells + 1,), jnp.int32)],
        [
            pltpu.VMEM((4, 128), jnp.int32),
            pltpu.SMEM((4, 128), jnp.int32),
            pltpu.VMEM((pairs + 1, FIELDS, 128), F32),
            pltpu.SemaphoreType.DMA,
        ],
        [spec(VMEM)],
        (got.reshape(peers * PEER_ROWS, 128),),
        out_specs=[spec(VMEM)] * 2 + [spec(SMEM)],
    )
    left, right = rims(head, tail)
    base = (rank * cells - rim).astype(jnp.int32).reshape(1)
    hi, lo, dens, coef_head, coef_tail = density(base, adj, count, left, head, tail, right)
    coef_left, coef_right = rims(coef_head, coef_tail)
    coefs = (coef_left, coef_head, coef_tail, coef_right)
    first_head, first_tail = sweep(
        True, base, adj, hi, lo, coefs, (left, head, tail, right), head, tail
    )
    first_left, first_right = rims(first_head, first_tail)
    speeds = (first_left, first_head, first_tail, first_right)
    (out,) = sweep(False, base, adj, hi, lo, coefs, speeds, head, tail)
    return out, dens.reshape(cells * SLOTS)


def solution(mesh):
    split, per_column = P("cells"), P(None, "cells")
    return jax.shard_map(
        body,
        mesh=mesh,
        in_specs=(per_column,) * 3 + (split,) * 6 + (per_column,),
        out_specs=(per_column, split),
        check_vma=False,
    )
```

```python
import functools

import jax
import jax.numpy as jnp
from jax import lax
from jax.experimental import pallas as pl
from jax.experimental.pallas import tpu as pltpu
from jax.sharding import PartitionSpec as P

SLOTS = 64
NEIGH = 27
ENTRY_ORDER = (13,) + tuple(range(13)) + tuple(range(14, 27))
ROWS = 14
WIDTH = ROWS * 128
CHUNK = 32
GROUP = 8
FIELDS = 8
PEER_ROWS = FIELDS + 1
TERMS = 32

step_time = 0.5
mass_rate = 0.3
visc_scale = 0.01
dens_scale = 0.01
heat_slope = 3.0
jamming_bound = 0.6

VMEM = pltpu.MemorySpace.VMEM
SMEM = pltpu.MemorySpace.SMEM
HBM = pltpu.MemorySpace.HBM
MIB = 1 << 20
BF16 = jnp.bfloat16
F32 = jnp.float32


def lane_iota(shape):
    return lax.broadcasted_iota(jnp.int32, shape, len(shape) - 1)


def sub_iota(shape):
    return lax.broadcasted_iota(jnp.int32, shape, len(shape) - 2)


def split_bf16(value, count):
    parts = []
    for _ in range(count):
        part = value.astype(BF16).astype(F32)
        parts.append(part)
        value = value - part
    return parts


def pack_kernel(*refs):
    inputs, sent, local, out, fields, seen, sems, out_sem = refs[:9], refs[9], refs[10:19], *refs[19:]
    copies = [pltpu.make_async_copy(a, b, sems.at[i]) for i, (a, b) in enumerate(zip(inputs, local))]
    for copy in copies:
        copy.start()
    tally, peer, place, pos, speed, force, weight, heat, share = local
    cells = tally.shape[0]
    peers = out.shape[0] // PEER_ROWS
    lane = lane_iota((1, 128))
    low = lane < SLOTS

    def clear(index, carry):
        seen[index] = 0
        out[pl.ds(index * PEER_ROWS + FIELDS, 1), :] = jnp.full((1, 128), -1.0, F32)
        return carry

    lax.fori_loop(0, peers, clear, 0, unroll=8)
    for copy in copies:
        copy.wait()
    open_bound = 1.0 - share[...] / jamming_bound
    resist = jnp.exp(heat_slope * heat[...]) * (open_bound * open_bound * jnp.sqrt(open_bound))
    for pair in range(cells // 2):
        span = pl.ds(pair * 128, 128)
        bound = jnp.where(low, tally[2 * pair], tally[2 * pair + 1] + SLOTS)
        live = (lane < bound).astype(F32)
        fields[pair, 0:3, :] = pos[:, span]
        fields[pair, 3:6, :] = speed[:, span] + step_time * force[:, span]
        fields[pair, 6:7, :] = weight[pair : pair + 1, :] * live
        fields[pair, 7:8, :] = resist[pair : pair + 1, :]
    half_of = lane_iota((FIELDS, 128)) // SLOTS

    def send(pair, carry):
        tile = fields[pair]
        turned = pltpu.roll(tile, SLOTS, 1)
        for side in range(2):
            cell = 2 * pair + side
            target = peer[cell]
            half = seen[target]
            seen[target] = 1
            row = target * PEER_ROWS
            value = jnp.where(half == side, tile, turned)
            pltpu.store(out.at[pl.ds(row, FIELDS), :], value, mask=half_of == half)
            first = half * SLOTS
            head = jnp.where(lane == first, place[cell].astype(F32), tally[cell].astype(F32))
            pltpu.store(
                out.at[pl.ds(row + FIELDS, 1), :], head, mask=(lane == first) | (lane == first + 1)
            )
        return carry

    lax.fori_loop(0, cells // 2, send, 0, unroll=4)
    copy = pltpu.make_async_copy(out, sent, out_sem)
    copy.start()
    copy.wait()


def unpack_kernel(got_hbm, head, tail, items, starts, count, heads_v, heads_s, store, got, sem):
    copy = pltpu.make_async_copy(got_hbm, got, sem)
    copy.start()
    copy.wait()
    peers = got.shape[0] // PEER_ROWS
    pairs = store.shape[0] - 1
    heads = jnp.transpose(got[pl.ds(FIELDS, peers, stride=PEER_ROWS), :])
    heads_v[0:2, :] = heads[0:2].astype(jnp.int32)
    heads_v[2:4, :] = heads[SLOTS : SLOTS + 2].astype(jnp.int32)
    copy = pltpu.make_async_copy(heads_v, heads_s, sem)
    copy.start()
    copy.wait()
    half_of = lane_iota((FIELDS, 128)) // SLOTS

    def take(source, carry):
        tile = got[pl.ds(source * PEER_ROWS, FIELDS), :]
        turned = pltpu.roll(tile, SLOTS, 1)
        for half in range(2):
            slot = heads_s[2 * half, source]
            slot = jnp.where(slot < 0, 2 * pairs, slot)
            count[slot] = heads_s[2 * half + 1, source]
            side = lax.rem(slot, 2)
            value = jnp.where(side == half, tile, turned)
            pltpu.store(store.at[slot // 2], value, mask=half_of == side)
        return carry

    lax.fori_loop(0, peers, take, 0, unroll=8)
    for index in range(items.shape[0]):
        items[index] = 0

    def list_items(cell, total):
        starts[cell] = total
        items[total] = 2 * cell
        items[total + 1] = 2 * cell + 1
        return total + 1 + (count[cell] > CHUNK).astype(jnp.int32)

    total = lax.fori_loop(0, 2 * pairs, list_items, 0, unroll=8)
    starts[2 * pairs] = (total + GROUP - 1) // GROUP
    head[...] = store[0 : pairs // 2]
    tail[...] = store[pairs // 2 : pairs]


def two_halves(tile, low):
    turned = pltpu.roll(tile, SLOTS, 1)
    return (tile, turned), low


def put_halves(tile, low, first, second, index):
    turned = pltpu.roll(tile, SLOTS, 1)
    zero = jnp.zeros_like(tile)
    first[index] = jnp.where(low, tile, zero).astype(first.dtype)
    second[index] = jnp.where(low, zero, turned).astype(first.dtype)
    first[index + 1] = jnp.where(low, turned, zero).astype(first.dtype)
    second[index + 1] = jnp.where(low, zero, tile).astype(first.dtype)


def over_items(groups, one_item):
    def turn(step, carry):
        for local in range(GROUP):
            one_item(step, local)
        return carry

    lax.fori_loop(0, groups, turn, 0)


def entries(adj, cell, dummy):
    return [adj[n, cell] for n in range(NEIGH)] + [dummy]


def density_kernel(
    items, starts, adj, left, head, tail, right, hi, lo, dens, coef_head, coef_tail,
    terms_a, terms_b, ext, stage, lhs, own_r, rows_t, rows_f, acc, raw,
):
    rim = 2 * head.shape[0]
    quarter = head.shape[0]
    dummy = 4 * rim
    low8 = lane_iota((FIELDS, 128)) < SLOTS
    low32 = lane_iota((TERMS, 128)) < SLOTS
    sub8 = sub_iota((FIELDS, 128))

    if True:
        ext[dummy] = jnp.where(sub8 == 7, 1.0, 0.0)
        terms_a[dummy] = jnp.zeros((TERMS, 128), BF16)
        terms_b[dummy] = jnp.zeros((TERMS, 128), BF16)
        ones = jnp.where(sub8 < 3, 1.0, 0.0)
        for part, ref in enumerate((left, head, tail, right)):
            for pair in range(quarter):
                tile = ref[pair]
                slot = part * rim + 2 * pair
                turned = pltpu.roll(tile, SLOTS, 1)
                ext[slot] = jnp.where(low8, tile, turned)
                ext[slot + 1] = jnp.where(low8, turned, tile)
                x, y, z = tile[0:1], tile[1:2], tile[2:3]
                length = x * x + y * y + z * z
                vector = jnp.where(sub8 == 3, -length, tile)
                v1, v2, v3 = split_bf16(vector, 3)
                at = slot // 2 % 8
                for row, v in enumerate((v1, v2, v3, v1, v2, v1)):
                    stage[at, 4 * row : 4 * row + 4, :] = v[0:4]
                stage[at, 24:32, :] = ones
                put_halves(stage[at], low32, terms_a, terms_b, slot)
                if part in (1, 2):
                    own = (part - 1) * quarter + pair
                    vector = jnp.where(sub8 == 3, 1.0, 2.0 * tile)
                    w1, w2, w3 = split_bf16(vector, 3)
                    a1, a2, a3 = split_bf16(1.0 - length, 3)
                    at = 8 + pair % 8
                    for row, w in enumerate((w1, w1, w1, w2, w2, w3)):
                        stage[at, 4 * row : 4 * row + 4, :] = w[0:4]
                    extra = jnp.where(sub8 == 0, a1, jnp.where(sub8 == 1, a2, a3))
                    stage[at, 24:32, :] = jnp.where(sub8 < 3, extra, tile[7:8])
                    turned = jnp.transpose(stage[at])
                    radius = jnp.broadcast_to(turned[:, 31:32], (128, 128))
                    lhs[4 * own : 4 * own + 4] = turned.astype(BF16).reshape(4, CHUNK, TERMS)
                    own_r[4 * own : 4 * own + 4] = radius.reshape(4, CHUNK, 128)

    chunk_lane = lane_iota((CHUNK, 128))
    chunk_sub = sub_iota((CHUNK, 128))

    def one_item(step, local):
        place = step * GROUP + local
        item = items[place]
        cell = item // 2
        at = local
        index = entries(adj, cell, dummy)
        for p in range(ROWS):
            i, j = index[2 * p], index[2 * p + 1]
            rows_f[at, p] = jnp.where(low8, ext[i], ext[j])
            rows_t[at, :, p * 128 : p * 128 + 128] = terms_a[i] + terms_b[j]
        own = lhs[item]
        ri = own_r[item]
        first = (item - 2 * cell) * CHUNK
        total = jnp.zeros((CHUNK, 128), F32)
        for p2 in range(ROWS // 2):
            wide = jnp.dot(
                own, rows_t[at, :, p2 * 256 : p2 * 256 + 256], preferred_element_type=F32
            )
            for p in (2 * p2, 2 * p2 + 1):
                q = jnp.maximum(wide[:, (p % 2) * 128 : (p % 2) * 128 + 128], 0.0)
                q2 = q * q
                total = total + q2 * (q * rows_f[at, p, 6:7, :])
                value = q2 * pl.reciprocal(ri + rows_f[at, p, 7:8, :])
                if p == 0:
                    value = jnp.where(chunk_lane == chunk_sub + first, 0.0, value)
                upper = value.astype(BF16)
                span = slice(p * 128, p * 128 + 128)
                hi[place, :, span] = upper
                lo[place, :, span] = (value - upper.astype(F32)).astype(BF16)
        acc[item] = total

    over_items(starts[4 * quarter], one_item)

    if True:
        ones = jnp.ones((FIELDS, 128), BF16)

        def reduce_pair(pair, carry):
            total = jnp.zeros((FIELDS, 128), F32)
            for part in split_bf16(acc[pl.ds(4 * pair, 4)].reshape(2 * SLOTS, 128), 3):
                total = total + lax.dot_general(
                    ones, part.astype(BF16), (((1,), (1,)), ((), ())), preferred_element_type=F32
                )
            raw[pl.ds(pair, 1), :] = total[0:1]
            return carry

        lax.fori_loop(0, 2 * quarter, reduce_pair, 0, unroll=4)
        for part, (ref, coef) in enumerate(((head, coef_head), (tail, coef_tail))):
            mass = ref[:, 6, :]
            live = mass > 0.0
            value = dens_scale * raw[part * quarter : (part + 1) * quarter, :]
            dens[part * quarter : (part + 1) * quarter, :] = jnp.where(live, value, 0.0)
            coef[...] = (2.0 * visc_scale) * mass / jnp.where(live, value, 1.0)


def sweep_kernel(is_first, items, starts, adj, hi, lo, *refs):
    coefs, speeds, refs = refs[:4], refs[4:8], refs[8:]
    if is_first:
        (head, tail), (out_head, out_tail), refs = speeds[1:3], refs[:2], refs[2:]
    else:
        (head, tail), (out,), refs = refs[:2], refs[2:3], refs[3:]
    ext_a, ext_b, rows, sums, stage = refs
    quarter = head.shape[0]
    rim = 2 * quarter
    dummy = 4 * rim
    low = lane_iota((FIELDS, 128)) < SLOTS
    low16 = lane_iota((2 * FIELDS, 128)) < SLOTS
    eighth = lane_iota((FIELDS, 128)) // CHUNK
    sub = sub_iota((FIELDS, 128))
    moving = (sub >= 3) & (sub < 6)

    if True:
        ext_a[dummy] = jnp.zeros((2 * FIELDS, 128), BF16)
        ext_b[dummy] = jnp.zeros((2 * FIELDS, 128), BF16)
        for part in range(4):
            for pair in range(quarter):
                tile = jnp.where(sub == 0, 1.0, jnp.where(moving, speeds[part][pair], 0.0))
                w1, w2 = split_bf16(tile * coefs[part][pair : pair + 1, :], 2)
                at = pair % 8
                stage[at, 0:FIELDS, :] = w1
                stage[at, FIELDS:, :] = w2
                put_halves(stage[at], low16, ext_a, ext_b, part * rim + 2 * pair)

    def one_item(step, local):
        place = step * GROUP + local
        index = entries(adj, items[place] // 2, dummy)
        at = local
        for p in range(ROWS):
            rows[at, :, p * 128 : p * 128 + 128] = ext_a[index[2 * p]] + ext_b[index[2 * p + 1]]
        total = jnp.zeros((2 * FIELDS, CHUNK), F32)
        for part in (hi, lo):
            total = total + lax.dot_general(
                rows[at], part[place], (((1,), (1,)), ((), ())), preferred_element_type=F32
            )
        sums[place, :, 0:CHUNK] = total[0:FIELDS] + total[FIELDS:]

    over_items(starts[2 * rim], one_item)

    if True:
        for part, ref in enumerate((head, tail)):
            for pair in range(quarter):
                slot = part * quarter + pair
                tile = ref[pair]
                total = sums[starts[2 * slot]]
                for n in range(1, 4):
                    place = starts[2 * slot + n // 2] + n % 2
                    total = jnp.where(eighth == n, pltpu.roll(sums[place], n * CHUNK, 1), total)
                live = jnp.broadcast_to(tile[6:7] > 0.0, (FIELDS, 128))
                rate = mass_rate * tile[6:7]
                below = jnp.broadcast_to(rate + total[0:1], (FIELDS, 128))
                value = (rate * tile + total) / jnp.where(live, below, 1.0)
                value = jnp.where(live & moving, value, 0.0)
                if is_first:
                    (out_head, out_tail)[part][pair] = value
                else:
                    out[:, slot * 128 : slot * 128 + 128] = value[3:6]


def call(kernel, outs, scratch, in_specs, args, out_specs, grid=(), scalars=0, vmem=40):
    return pl.pallas_call(
        kernel,
        out_shape=outs,
        grid_spec=pltpu.PrefetchScalarGridSpec(
            num_scalar_prefetch=scalars,
            grid=grid,
            in_specs=in_specs,
            out_specs=out_specs,
            scratch_shapes=scratch,
        ),
        compiler_params=pltpu.CompilerParams(vmem_limit_bytes=vmem * MIB),
    )(*args)


def f32(*shape):
    return jax.ShapeDtypeStruct(shape, F32)


def spec(space):
    return pl.BlockSpec(memory_space=space)


def whole(*shape):
    return pl.BlockSpec(shape, lambda *scalars: (0,) * len(shape))


def density(items, starts, adj, left, head, tail, right):
    quarter = head.shape[0]
    cells, pairs = 4 * quarter, 2 * quarter
    ext = 2 * cells + 1
    tile = whole(quarter, FIELDS, 128)
    block = spec(VMEM)
    return call(
        density_kernel,
        [pltpu.VMEM((2 * cells, CHUNK, WIDTH), BF16)] * 2
        + [f32(pairs, 128), f32(quarter, 128), f32(quarter, 128)],
        [pltpu.VMEM((ext, TERMS, 128), BF16)] * 2
        + [
            pltpu.VMEM((ext, FIELDS, 128), F32),
            pltpu.VMEM((16, TERMS, 128), F32),
            pltpu.VMEM((2 * cells, CHUNK, TERMS), BF16),
            pltpu.VMEM((2 * cells, CHUNK, 128), F32),
            pltpu.VMEM((GROUP, TERMS, WIDTH), BF16),
            pltpu.VMEM((GROUP, ROWS, FIELDS, 128), F32),
            pltpu.VMEM((2 * cells, CHUNK, 128), F32),
            pltpu.VMEM((pairs, 128), F32),
        ],
        [tile] * 4,
        (items, starts, adj, left, head, tail, right),
        out_specs=[block] * 2 + [whole(pairs, 128), whole(quarter, 128), whole(quarter, 128)],
        vmem=22,
        scalars=3,
    )


def sweep(is_first, items, starts, adj, hi, lo, coefs, speeds, head, tail):
    quarter = head.shape[0]
    cells = 4 * quarter
    ext = 2 * cells + 1
    tile = whole(quarter, FIELDS, 128)
    block = spec(VMEM)
    own = () if is_first else (head, tail)
    if is_first:
        outs, out_specs = [f32(quarter, FIELDS, 128)] * 2, [tile] * 2
    else:
        outs, out_specs = [f32(3, cells * SLOTS)], [whole(3, cells * SLOTS)]
    return call(
        functools.partial(sweep_kernel, is_first),
        outs,
        [pltpu.VMEM((ext, 2 * FIELDS, 128), BF16)] * 2
        + [
            pltpu.VMEM((GROUP, 2 * FIELDS, WIDTH), BF16),
            pltpu.VMEM((2 * cells + GROUP, FIELDS, 128), F32),
            pltpu.VMEM((8, 2 * FIELDS, 128), F32),
        ],
        [block] * 2 + [whole(quarter, 128)] * 4 + [tile] * (4 + len(own)),
        (items, starts, adj, hi, lo) + tuple(coefs) + tuple(speeds) + own,
        out_specs=out_specs,
        vmem=22,
        scalars=3,
    )


def body(pos, speed, force, weight, heat, share, tally, peer, place, adj):
    peers = lax.axis_size("cells")
    rank = lax.axis_index("cells")
    cells = tally.shape[0]
    rim = cells // 2
    quarter = cells // 4
    pairs = cells // 2
    right_going = [(i, i + 1) for i in range(peers - 1)]
    left_going = [(i + 1, i) for i in range(peers - 1)]

    def rims(head, tail):
        return lax.ppermute(tail, "cells", right_going), lax.ppermute(head, "cells", left_going)

    args = (tally, peer, place, pos, speed, force)
    args = args + tuple(v.reshape(pairs, 128) for v in (weight, heat, share))
    args = tuple(pltpu.with_memory_space_constraint(v, HBM) for v in args)
    (sent,) = call(
        pack_kernel,
        [pltpu.HBM((peers * PEER_ROWS, 128), F32)],
        [(pltpu.SMEM if i < 3 else pltpu.VMEM)(v.shape, v.dtype) for i, v in enumerate(args)]
        + [
            pltpu.VMEM((peers * PEER_ROWS, 128), F32),
            pltpu.VMEM((pairs, FIELDS, 128), F32),
            pltpu.SMEM((peers,), jnp.int32),
            pltpu.SemaphoreType.DMA((9,)),
            pltpu.SemaphoreType.DMA,
        ],
        [spec(HBM)] * 9,
        args,
        out_specs=[spec(HBM)],
    )
    got = lax.all_to_all(
        sent.reshape(peers, 1, PEER_ROWS * 128), "cells", split_axis=0, concat_axis=0, tiled=True
    )
    head, tail, items, starts = call(
        unpack_kernel,
        [f32(quarter, FIELDS, 128)] * 2
        + [jax.ShapeDtypeStruct((n,), jnp.int32) for n in (2 * cells + GROUP, cells + 1)],
        [
            pltpu.SMEM((cells + 1,), jnp.int32),
            pltpu.VMEM((4, 128), jnp.int32),
            pltpu.SMEM((4, 128), jnp.int32),
            pltpu.VMEM((pairs + 1, FIELDS, 128), F32),
            pltpu.VMEM((peers * PEER_ROWS, 128), F32),
            pltpu.SemaphoreType.DMA,
        ],
        [spec(HBM)],
        (got.reshape(peers * PEER_ROWS, 128),),
        out_specs=[spec(VMEM)] * 2 + [spec(SMEM)] * 2,
    )
    left, right = rims(head, tail)
    local = adj - (rank * cells - rim).astype(jnp.int32)
    adj = jnp.concatenate([local[13:14], local[:13], local[14:]], axis=0)
    hi, lo, dens, coef_head, coef_tail = density(items, starts, adj, left, head, tail, right)
    hi, lo = (pltpu.with_memory_space_constraint(v, VMEM) for v in (hi, lo))
    coef_left, coef_right = rims(coef_head, coef_tail)
    coefs = (coef_left, coef_head, coef_tail, coef_right)
    first_head, first_tail = sweep(
        True, items, starts, adj, hi, lo, coefs, (left, head, tail, right), head, tail
    )
    first_left, first_right = rims(first_head, first_tail)
    speeds = (first_left, first_head, first_tail, first_right)
    (out,) = sweep(False, items, starts, adj, hi, lo, coefs, speeds, head, tail)
    return out, dens.reshape(cells * SLOTS)


def solution(mesh):
    split, per_column = P("cells"), P(None, "cells")
    return jax.shard_map(
        body,
        mesh=mesh,
        in_specs=(per_column,) * 3 + (split,) * 6 + (per_column,),
        out_specs=(per_column, split),
        check_vma=False,
    )
```

```python
import functools

import jax
import jax.numpy as jnp
from jax import lax
from jax.experimental import pallas as pl
from jax.experimental.pallas import tpu as pltpu
from jax.sharding import PartitionSpec as P

SLOTS = 64
NEIGH = 27
ENTRY_ORDER = (13,) + tuple(range(13)) + tuple(range(14, 27))
ROWS = 14
WIDTH = ROWS * 128
CHUNK = 32
GROUP = 8
QUAD = 4
FIELDS = 8
PEER_ROWS = FIELDS + 1
TERMS = 32

step_time = 0.5
mass_rate = 0.3
visc_scale = 0.01
dens_scale = 0.01
heat_slope = 3.0
jamming_bound = 0.6

VMEM = pltpu.MemorySpace.VMEM
SMEM = pltpu.MemorySpace.SMEM
HBM = pltpu.MemorySpace.HBM
MIB = 1 << 20
BF16 = jnp.bfloat16
F32 = jnp.float32


def lane_iota(shape):
    return lax.broadcasted_iota(jnp.int32, shape, len(shape) - 1)


def sub_iota(shape):
    return lax.broadcasted_iota(jnp.int32, shape, len(shape) - 2)


def split_bf16(value, count):
    parts = []
    for _ in range(count):
        part = value.astype(BF16).astype(F32)
        parts.append(part)
        value = value - part
    return parts


def pack_kernel(*refs):
    inputs, sent, local, out, fields, seen, sems, out_sem = refs[:9], refs[9], refs[10:19], *refs[19:]
    copies = [pltpu.make_async_copy(a, b, sems.at[i]) for i, (a, b) in enumerate(zip(inputs, local))]
    for copy in copies:
        copy.start()
    tally, peer, place, pos, speed, force, weight, heat, share = local
    cells = tally.shape[0]
    peers = out.shape[0] // PEER_ROWS
    lane = lane_iota((1, 128))
    low = lane < SLOTS

    def clear(index, carry):
        seen[index] = 0
        out[pl.ds(index * PEER_ROWS + FIELDS, 1), :] = jnp.full((1, 128), -1.0, F32)
        return carry

    lax.fori_loop(0, peers, clear, 0, unroll=8)
    for copy in copies:
        copy.wait()
    open_bound = 1.0 - share[...] / jamming_bound
    resist = jnp.exp(heat_slope * heat[...]) * (open_bound * open_bound * jnp.sqrt(open_bound))
    for pair in range(cells // 2):
        span = pl.ds(pair * 128, 128)
        bound = jnp.where(low, tally[2 * pair], tally[2 * pair + 1] + SLOTS)
        live = (lane < bound).astype(F32)
        fields[pair, 0:3, :] = pos[:, span]
        fields[pair, 3:6, :] = speed[:, span] + step_time * force[:, span]
        fields[pair, 6:7, :] = weight[pair : pair + 1, :] * live
        fields[pair, 7:8, :] = resist[pair : pair + 1, :]
    half_of = lane_iota((FIELDS, 128)) // SLOTS

    def send(pair, carry):
        tile = fields[pair]
        turned = pltpu.roll(tile, SLOTS, 1)
        for side in range(2):
            cell = 2 * pair + side
            target = peer[cell]
            half = seen[target]
            seen[target] = 1
            row = target * PEER_ROWS
            value = jnp.where(half == side, tile, turned)
            pltpu.store(out.at[pl.ds(row, FIELDS), :], value, mask=half_of == half)
            first = half * SLOTS
            head = jnp.where(lane == first, place[cell].astype(F32), tally[cell].astype(F32))
            pltpu.store(
                out.at[pl.ds(row + FIELDS, 1), :], head, mask=(lane == first) | (lane == first + 1)
            )
        return carry

    lax.fori_loop(0, cells // 2, send, 0, unroll=4)
    copy = pltpu.make_async_copy(out, sent, out_sem)
    copy.start()
    copy.wait()


def list_kernel(count, fulls, halves, starts):
    cells = starts.shape[0] - 2
    for index in range(fulls.shape[0]):
        fulls[index] = 0
    for index in range(halves.shape[0]):
        halves[index] = 0

    def list_cell(cell, carry):
        full, half = carry
        fulls[full] = cell
        halves[half] = cell
        more = (count[cell] > CHUNK).astype(jnp.int32)
        starts[cell] = jnp.where(more > 0, 2 * full, -1 - half)
        return full + more, half + 1 - more

    full, half = lax.fori_loop(0, cells, list_cell, (0, 0), unroll=8)
    full_turns = (2 * full + GROUP - 1) // GROUP
    starts[cells] = full_turns
    starts[cells + 1] = (half + GROUP - 1) // GROUP

    def shift_cell(cell, carry):
        start = starts[cell]
        starts[cell] = jnp.where(start < 0, GROUP * full_turns - 1 - start, start)
        return carry

    lax.fori_loop(0, cells, shift_cell, 0, unroll=8)


def unpack_kernel(got_hbm, head, tail, count, heads_v, heads_s, store, got, sem):
    copy = pltpu.make_async_copy(got_hbm, got, sem)
    copy.start()
    copy.wait()
    peers = got.shape[0] // PEER_ROWS
    pairs = store.shape[0] - 1
    heads = jnp.transpose(got[pl.ds(FIELDS, peers, stride=PEER_ROWS), :])
    heads_v[0:2, :] = heads[0:2].astype(jnp.int32)
    heads_v[2:4, :] = heads[SLOTS : SLOTS + 2].astype(jnp.int32)
    copy = pltpu.make_async_copy(heads_v, heads_s, sem)
    copy.start()
    copy.wait()
    half_of = lane_iota((FIELDS, 128)) // SLOTS

    def take(source, carry):
        tile = got[pl.ds(source * PEER_ROWS, FIELDS), :]
        turned = pltpu.roll(tile, SLOTS, 1)
        for half in range(2):
            slot = heads_s[2 * half, source]
            slot = jnp.where(slot < 0, 2 * pairs, slot)
            count[slot] = heads_s[2 * half + 1, source]
            side = lax.rem(slot, 2)
            value = jnp.where(side == half, tile, turned)
            pltpu.store(store.at[slot // 2], value, mask=half_of == side)
        return carry

    lax.fori_loop(0, peers, take, 0, unroll=8)
    head[...] = store[0 : pairs // 2]
    tail[...] = store[pairs // 2 : pairs]


def two_halves(tile, low):
    turned = pltpu.roll(tile, SLOTS, 1)
    return (tile, turned), low


def put_halves(tile, low, first, second, index):
    turned = pltpu.roll(tile, SLOTS, 1)
    zero = jnp.zeros_like(tile)
    first[index] = jnp.where(low, tile, zero).astype(first.dtype)
    second[index] = jnp.where(low, zero, turned).astype(first.dtype)
    first[index + 1] = jnp.where(low, turned, zero).astype(first.dtype)
    second[index + 1] = jnp.where(low, zero, tile).astype(first.dtype)


def lane_sums(picks, value):
    total = jnp.zeros((FIELDS, value.shape[0]), F32)
    for part in split_bf16(value, 2):
        total = total + lax.dot_general(
            picks, part.astype(BF16), (((1,), (1,)), ((), ())), preferred_element_type=F32
        )
    return total


def over_items(lists, cells, one_cell, acc, sums, picks):
    fulls, halves, starts = lists
    full_turns = starts[cells]
    quads = GROUP // QUAD

    def add_up(step):
        for n in range(quads):
            sums[step * quads + n] = lane_sums(picks, acc[step * quads + n])

    def turns(chosen, each, skipped):
        def turn(step, carry):
            add_up(jnp.maximum(skipped + step - 1, 0))
            place = (skipped + step) * GROUP
            values = []
            for local in range(GROUP // each):
                cell = chosen[step * (GROUP // each) + local]
                values += one_cell(cell, place + each * local, local, each)
            for n, value in enumerate(values):
                acc[(skipped + step) * quads + n // QUAD, n % QUAD * CHUNK : n % QUAD * CHUNK + CHUNK, :] = value
            return carry

        return turn

    lax.fori_loop(0, full_turns, turns(fulls, 2, 0), 0)
    lax.fori_loop(0, starts[cells + 1], turns(halves, 1, full_turns), 0)
    add_up(full_turns + starts[cells + 1] - 1)


def pair_sums(sums, starts, pair, group):
    total = None
    for n in range(4):
        place = starts[2 * pair + n // 2] + n % 2
        tile = pltpu.roll(sums[place // QUAD], ((n - place) & 3) * CHUNK, 1)
        total = tile if total is None else jnp.where(group == n, tile, total)
    return total


def entries(adj, cell, dummy):
    return [adj[n, cell] for n in range(NEIGH)] + [dummy]


def density_kernel(
    fulls, halves, starts, adj, left, head, tail, right, h, dens, coef_head, coef_tail,
    terms_a, terms_b, ext, stage, lhs, own_r, rows_t, rows_f, acc, sums, raw,
):
    rim = 2 * head.shape[0]
    quarter = head.shape[0]
    dummy = 4 * rim
    low8 = lane_iota((FIELDS, 128)) < SLOTS
    low32 = lane_iota((TERMS, 128)) < SLOTS
    sub8 = sub_iota((FIELDS, 128))

    if True:
        ext[dummy] = jnp.where(sub8 == 7, 1.0, 0.0)
        terms_a[dummy] = jnp.zeros((TERMS, 128), BF16)
        terms_b[dummy] = jnp.zeros((TERMS, 128), BF16)
        ones = jnp.where(sub8 < 3, 1.0, 0.0)
        for part, ref in enumerate((left, head, tail, right)):
            for pair in range(quarter):
                tile = ref[pair]
                slot = part * rim + 2 * pair
                turned = pltpu.roll(tile, SLOTS, 1)
                ext[slot] = jnp.where(low8, tile, turned)
                ext[slot + 1] = jnp.where(low8, turned, tile)
                x, y, z = tile[0:1], tile[1:2], tile[2:3]
                length = x * x + y * y + z * z
                vector = jnp.where(sub8 == 3, -length, tile)
                v1, v2, v3 = split_bf16(vector, 3)
                at = slot // 2 % 8
                for row, v in enumerate((v1, v2, v3, v1, v2, v1)):
                    stage[at, 4 * row : 4 * row + 4, :] = v[0:4]
                stage[at, 24:32, :] = ones
                put_halves(stage[at], low32, terms_a, terms_b, slot)
                if part in (1, 2):
                    own = (part - 1) * quarter + pair
                    vector = jnp.where(sub8 == 3, 1.0, 2.0 * tile)
                    w1, w2, w3 = split_bf16(vector, 3)
                    a1, a2, a3 = split_bf16(1.0 - length, 3)
                    at = 8 + pair % 8
                    for row, w in enumerate((w1, w1, w1, w2, w2, w3)):
                        stage[at, 4 * row : 4 * row + 4, :] = w[0:4]
                    extra = jnp.where(sub8 == 0, a1, jnp.where(sub8 == 1, a2, a3))
                    stage[at, 24:32, :] = jnp.where(sub8 < 3, extra, tile[7:8])
                    turned = jnp.transpose(stage[at])
                    radius = jnp.broadcast_to(turned[:, 31:32], (128, 128))
                    lhs[2 * own : 2 * own + 2] = turned.astype(BF16).reshape(2, SLOTS, TERMS)
                    own_r[2 * own : 2 * own + 2] = radius.reshape(2, SLOTS, 128)

    item_lane = lane_iota((CHUNK, 128))
    item_sub = sub_iota((CHUNK, 128))

    def one_cell(cell, place, at, each):
        index = entries(adj, cell, dummy)
        for p in range(ROWS):
            i, j = index[2 * p], index[2 * p + 1]
            rows_f[at, p] = jnp.where(low8, ext[i], ext[j])
            rows_t[at, :, p * 128 : p * 128 + 128] = terms_a[i] + terms_b[j]
        own = lhs[cell, 0 : each * CHUNK]
        totals = [jnp.zeros((CHUNK, 128), F32) for _ in range(each)]
        for p2 in range(ROWS // 2):
            wide = jnp.dot(
                own, rows_t[at, :, p2 * 256 : p2 * 256 + 256], preferred_element_type=F32
            )
            for p in (2 * p2, 2 * p2 + 1):
                for part in range(each):
                    first = part * CHUNK
                    q = wide[first : first + CHUNK, (p % 2) * 128 : (p % 2) * 128 + 128]
                    q = jnp.maximum(q, 0.0)
                    q2 = q * q
                    totals[part] = totals[part] + q2 * (q * rows_f[at, p, 6:7, :])
                    ri = own_r[cell, first : first + CHUNK]
                    value = q2 * pl.reciprocal(ri + rows_f[at, p, 7:8, :])
                    if p == 0:
                        value = jnp.where(item_lane == item_sub + first, 0.0, value)
                    h[place + part, p] = value
        return totals

    over_items((fulls, halves, starts), 4 * quarter, one_cell, acc, sums, jnp.ones((FIELDS, 128), BF16))

    if True:
        group = lane_iota((FIELDS, 128)) // CHUNK
        for pair in range(2 * quarter):
            total = pair_sums(sums, starts, pair, group)
            raw[pair : pair + 1, :] = total[0:1]
        for part, (ref, coef) in enumerate(((head, coef_head), (tail, coef_tail))):
            mass = ref[:, 6, :]
            live = mass > 0.0
            value = dens_scale * raw[part * quarter : (part + 1) * quarter, :]
            dens[part * quarter : (part + 1) * quarter, :] = jnp.where(live, value, 0.0)
            coef[...] = (2.0 * visc_scale) * mass / jnp.where(live, value, 1.0)


def sweep_kernel(is_first, fulls, halves, starts, adj, h, *refs):
    coefs, speeds, refs = refs[:4], refs[4:8], refs[8:]
    if is_first:
        (head, tail), (out_head, out_tail, below), refs = speeds[1:3], refs[:3], refs[3:]
    else:
        (head, tail, below), (out,), refs = refs[:3], refs[3:4], refs[4:]
    ext, rows, acc, sums = refs
    quarter = head.shape[0]
    rim = 2 * quarter
    dummy = 4 * rim
    lane = lane_iota((FIELDS, 128))
    low = lane < SLOTS
    sub = sub_iota((FIELDS, 128))
    moving = (sub >= 3) & (sub < 6)
    ext[dummy] = jnp.zeros((FIELDS, 128), F32)
    for part in range(4):
        for pair in range(quarter):
            tile = jnp.where(sub == 2, 1.0, jnp.where(moving, speeds[part][pair], 0.0))
            tile = tile * coefs[part][pair : pair + 1, :]
            turned = pltpu.roll(tile, SLOTS, 1)
            slot = part * rim + 2 * pair
            ext[slot] = jnp.where(low, tile, turned)
            ext[slot + 1] = jnp.where(low, turned, tile)
    order = (3, 5, 4, 2)
    item_group = lane_iota((CHUNK, 128)) // CHUNK
    item_low = item_group < 2
    item_even = item_group % 2 == 0

    def merge(a, b):
        if b is None:
            return a + pltpu.roll(a, 64, 1)
        return jnp.where(item_low, a, b) + pltpu.roll(jnp.where(item_low, b, a), 64, 1)

    def one_cell(cell, place, at, each):
        index = entries(adj, cell, dummy)
        for p in range(ROWS):
            rows[at, p] = jnp.where(low, ext[index[2 * p]], ext[index[2 * p + 1]])
        merged = []
        for part in range(each):
            totals = [jnp.zeros((CHUNK, 128), F32) for _ in order]
            for p in range(ROWS):
                value = h[place + part, p]
                for n, f in enumerate(order):
                    if is_first or f != 2:
                        totals[n] = totals[n] + value * rows[at, p, f : f + 1, :]
            even = merge(totals[0], totals[2])
            odd = merge(totals[1], totals[3] if is_first else None)
            other = jnp.where(item_even, odd, even)
            moved = jnp.where(item_even, pltpu.roll(other, 96, 1), pltpu.roll(other, 32, 1))
            merged.append(jnp.where(item_even, even, odd) + moved)
        return merged

    group = lane // CHUNK
    picks = jnp.zeros((FIELDS, 128), jnp.bool_)
    for n, f in enumerate(order):
        picks = picks | ((group == n) & (sub == f))
    picks = picks.astype(F32).astype(BF16)
    over_items((fulls, halves, starts), 2 * rim, one_cell, acc, sums, picks)
    for part, ref in enumerate((head, tail)):
        for pair in range(quarter):
            slot = part * quarter + pair
            tile = ref[pair]
            total = pair_sums(sums, starts, slot, group)
            if is_first:
                weight = total[2:3]
                below[slot : slot + 1, :] = weight
            else:
                weight = below[slot : slot + 1, :]
            live = jnp.broadcast_to(tile[6:7] > 0.0, (FIELDS, 128))
            rate = mass_rate * tile[6:7]
            under = jnp.broadcast_to(rate + weight, (FIELDS, 128))
            value = (rate * tile + total) / jnp.where(live, under, 1.0)
            value = jnp.where(live & moving, value, 0.0)
            if is_first:
                (out_head, out_tail)[part][pair] = value
            else:
                out[:, slot * 128 : slot * 128 + 128] = value[3:6]


def call(kernel, outs, scratch, in_specs, args, out_specs, grid=(), scalars=0, vmem=40):
    return pl.pallas_call(
        kernel,
        out_shape=outs,
        grid_spec=pltpu.PrefetchScalarGridSpec(
            num_scalar_prefetch=scalars,
            grid=grid,
            in_specs=in_specs,
            out_specs=out_specs,
            scratch_shapes=scratch,
        ),
        compiler_params=pltpu.CompilerParams(vmem_limit_bytes=vmem * MIB),
    )(*args)


def f32(*shape):
    return jax.ShapeDtypeStruct(shape, F32)


def spec(space):
    return pl.BlockSpec(memory_space=space)


def whole(*shape):
    return pl.BlockSpec(shape, lambda *scalars: (0,) * len(shape))


def density(lists, adj, left, head, tail, right):
    quarter = head.shape[0]
    cells, pairs = 4 * quarter, 2 * quarter
    ext = 2 * cells + 1
    tile = whole(quarter, FIELDS, 128)
    block = spec(VMEM)
    return call(
        density_kernel,
        [pltpu.VMEM((2 * cells + GROUP, ROWS, CHUNK, 128), F32)]
        + [f32(pairs, 128), f32(quarter, 128), f32(quarter, 128)],
        [pltpu.VMEM((ext, TERMS, 128), BF16)] * 2
        + [
            pltpu.VMEM((ext, FIELDS, 128), F32),
            pltpu.VMEM((16, TERMS, 128), F32),
            pltpu.VMEM((cells, SLOTS, TERMS), BF16),
            pltpu.VMEM((cells, SLOTS, 128), F32),
            pltpu.VMEM((GROUP, TERMS, WIDTH), BF16),
            pltpu.VMEM((GROUP, ROWS, FIELDS, 128), F32),
            pltpu.VMEM(((2 * cells + GROUP) // QUAD, 128, 128), F32),
            pltpu.VMEM(((2 * cells + GROUP) // QUAD + 1, FIELDS, 128), F32),
            pltpu.VMEM((pairs, 128), F32),
        ],
        [spec(VMEM)] * 4,
        (*lists, adj, left, head, tail, right),
        out_specs=[block] + [whole(pairs, 128), whole(quarter, 128), whole(quarter, 128)],
        vmem=22,
        scalars=4,
    )


def sweep(is_first, lists, adj, h, coefs, speeds, own):
    quarter = speeds[0].shape[0]
    cells, pairs = 4 * quarter, 2 * quarter
    ext = 2 * cells + 1
    tile = whole(quarter, FIELDS, 128)
    own_specs = [tile, tile, whole(pairs, 128)][: len(own)]
    if is_first:
        outs = [f32(quarter, FIELDS, 128)] * 2 + [f32(pairs, 128)]
        out_specs = [tile] * 2 + [whole(pairs, 128)]
    else:
        outs, out_specs = [f32(3, cells * SLOTS)], [whole(3, cells * SLOTS)]
    return call(
        functools.partial(sweep_kernel, is_first),
        outs,
        [
            pltpu.VMEM((ext, FIELDS, 128), F32),
            pltpu.VMEM((GROUP, ROWS, FIELDS, 128), F32),
            pltpu.VMEM(((2 * cells + GROUP) // QUAD, 128, 128), F32),
            pltpu.VMEM(((2 * cells + GROUP) // QUAD + 1, FIELDS, 128), F32),
        ],
        [spec(VMEM)] * (9 + len(own)),
        (*lists, adj, h) + tuple(coefs) + tuple(speeds) + own,
        out_specs=out_specs,
        vmem=22,
        scalars=4,
    )


def body(pos, speed, force, weight, heat, share, tally, peer, place, adj):
    peers = lax.axis_size("cells")
    rank = lax.axis_index("cells")
    cells = tally.shape[0]
    rim = cells // 2
    quarter = cells // 4
    pairs = cells // 2
    right_going = [(i, i + 1) for i in range(peers - 1)]
    left_going = [(i + 1, i) for i in range(peers - 1)]

    def rims(head, tail):
        return lax.ppermute(tail, "cells", right_going), lax.ppermute(head, "cells", left_going)

    args = (tally, peer, place, pos, speed, force)
    args = args + tuple(v.reshape(pairs, 128) for v in (weight, heat, share))
    args = tuple(pltpu.with_memory_space_constraint(v, HBM) for v in args)
    (sent,) = call(
        pack_kernel,
        [pltpu.HBM((peers * PEER_ROWS, 128), F32)],
        [(pltpu.SMEM if i < 3 else pltpu.VMEM)(v.shape, v.dtype) for i, v in enumerate(args)]
        + [
            pltpu.VMEM((peers * PEER_ROWS, 128), F32),
            pltpu.VMEM((pairs, FIELDS, 128), F32),
            pltpu.SMEM((peers,), jnp.int32),
            pltpu.SemaphoreType.DMA((9,)),
            pltpu.SemaphoreType.DMA,
        ],
        [spec(HBM)] * 9,
        args,
        out_specs=[spec(HBM)],
    )
    got = lax.all_to_all(
        sent.reshape(peers, 1, PEER_ROWS * 128), "cells", split_axis=0, concat_axis=0, tiled=True
    )
    head, tail, count = call(
        unpack_kernel,
        [f32(quarter, FIELDS, 128)] * 2
        + [jax.ShapeDtypeStruct((cells + 1,), jnp.int32)],
        [
            pltpu.VMEM((4, 128), jnp.int32),
            pltpu.SMEM((4, 128), jnp.int32),
            pltpu.VMEM((pairs + 1, FIELDS, 128), F32),
            pltpu.VMEM((peers * PEER_ROWS, 128), F32),
            pltpu.SemaphoreType.DMA,
        ],
        [spec(HBM)],
        (got.reshape(peers * PEER_ROWS, 128),),
        out_specs=[spec(VMEM)] * 2 + [spec(SMEM)],
    )
    left, right = rims(head, tail)
    lists = call(
        list_kernel,
        [jax.ShapeDtypeStruct((n,), jnp.int32) for n in (cells + GROUP, cells + GROUP, cells + 2)],
        [],
        [spec(SMEM)],
        (count,),
        out_specs=[spec(SMEM)] * 3,
    )
    local = adj - (rank * cells - rim).astype(jnp.int32)
    adj = jnp.concatenate([local[13:14], local[:13], local[14:]], axis=0)
    h, dens, coef_head, coef_tail = density(lists, adj, left, head, tail, right)
    h = pltpu.with_memory_space_constraint(h, VMEM)
    coef_left, coef_right = rims(coef_head, coef_tail)
    coefs = (coef_left, coef_head, coef_tail, coef_right)
    first_head, first_tail, below = sweep(
        True, lists, adj, h, coefs, (left, head, tail, right), ()
    )
    first_left, first_right = rims(first_head, first_tail)
    speeds = (first_left, first_head, first_tail, first_right)
    (out,) = sweep(False, lists, adj, h, coefs, speeds, (head, tail, below))
    return out, dens.reshape(cells * SLOTS)


def solution(mesh):
    split, per_column = P("cells"), P(None, "cells")
    return jax.shard_map(
        body,
        mesh=mesh,
        in_specs=(per_column,) * 3 + (split,) * 6 + (per_column,),
        out_specs=(per_column, split),
        check_vma=False,
    )
```

```python
import functools

import jax
import jax.numpy as jnp
from jax import lax
from jax.experimental import pallas as pl
from jax.experimental.pallas import tpu as pltpu
from jax.sharding import PartitionSpec as P

SLOTS = 64
NEIGH = 27
ENTRY_ORDER = (13,) + tuple(range(13)) + tuple(range(14, 27))
ROWS = 14
WIDTH = ROWS * 128
CHUNK = 32
GROUP = 8
QUAD = 4
FIELDS = 8
PEER_ROWS = FIELDS + 1
TERMS = 32

step_time = 0.5
mass_rate = 0.3
visc_scale = 0.01
dens_scale = 0.01
heat_slope = 3.0
jamming_bound = 0.6

VMEM = pltpu.MemorySpace.VMEM
SMEM = pltpu.MemorySpace.SMEM
HBM = pltpu.MemorySpace.HBM
MIB = 1 << 20
BF16 = jnp.bfloat16
F32 = jnp.float32


def lane_iota(shape):
    return lax.broadcasted_iota(jnp.int32, shape, len(shape) - 1)


def sub_iota(shape):
    return lax.broadcasted_iota(jnp.int32, shape, len(shape) - 2)


def split_bf16(value, count):
    parts = []
    for _ in range(count):
        part = value.astype(BF16).astype(F32)
        parts.append(part)
        value = value - part
    return parts


def pack_kernel(*refs):
    inputs, sent, local, out, fields, seen, sems, out_sem = refs[:9], refs[9], refs[10:19], *refs[19:]
    copies = [pltpu.make_async_copy(a, b, sems.at[i]) for i, (a, b) in enumerate(zip(inputs, local))]
    for copy in copies:
        copy.start()
    tally, peer, place, pos, speed, force, weight, heat, share = local
    cells = tally.shape[0]
    peers = out.shape[0] // PEER_ROWS
    lane = lane_iota((1, 128))
    low = lane < SLOTS

    def clear(index, carry):
        seen[index] = 0
        out[pl.ds(index * PEER_ROWS + FIELDS, 1), :] = jnp.full((1, 128), -1.0, F32)
        return carry

    lax.fori_loop(0, peers, clear, 0, unroll=8)
    for copy in copies:
        copy.wait()
    open_bound = 1.0 - share[...] / jamming_bound
    resist = jnp.exp(heat_slope * heat[...]) * (open_bound * open_bound * jnp.sqrt(open_bound))
    for pair in range(cells // 2):
        span = pl.ds(pair * 128, 128)
        bound = jnp.where(low, tally[2 * pair], tally[2 * pair + 1] + SLOTS)
        live = (lane < bound).astype(F32)
        fields[pair, 0:3, :] = pos[:, span]
        fields[pair, 3:6, :] = speed[:, span] + step_time * force[:, span]
        fields[pair, 6:7, :] = weight[pair : pair + 1, :] * live
        fields[pair, 7:8, :] = resist[pair : pair + 1, :]
    half_of = lane_iota((FIELDS, 128)) // SLOTS

    def send(pair, carry):
        tile = fields[pair]
        turned = pltpu.roll(tile, SLOTS, 1)
        for side in range(2):
            cell = 2 * pair + side
            target = peer[cell]
            half = seen[target]
            seen[target] = 1
            row = target * PEER_ROWS
            value = jnp.where(half == side, tile, turned)
            pltpu.store(out.at[pl.ds(row, FIELDS), :], value, mask=half_of == half)
            first = half * SLOTS
            head = jnp.where(lane == first, place[cell].astype(F32), tally[cell].astype(F32))
            pltpu.store(
                out.at[pl.ds(row + FIELDS, 1), :], head, mask=(lane == first) | (lane == first + 1)
            )
        return carry

    lax.fori_loop(0, cells // 2, send, 0, unroll=8)
    copy = pltpu.make_async_copy(out, sent, out_sem)
    copy.start()
    copy.wait()


def list_kernel(count, fulls, halves, starts):
    cells = starts.shape[0] - 2
    for index in range(fulls.shape[0]):
        fulls[index] = 0
    for index in range(halves.shape[0]):
        halves[index] = 0

    def list_cell(cell, carry):
        full, half = carry
        fulls[full] = cell
        halves[half] = cell
        more = (count[cell] > CHUNK).astype(jnp.int32)
        starts[cell] = jnp.where(more > 0, 2 * full, -1 - half)
        return full + more, half + 1 - more

    full, half = lax.fori_loop(0, cells, list_cell, (0, 0), unroll=8)
    full_turns = (2 * full + GROUP - 1) // GROUP
    starts[cells] = full_turns
    starts[cells + 1] = (half + GROUP - 1) // GROUP

    def shift_cell(cell, carry):
        start = starts[cell]
        starts[cell] = jnp.where(start < 0, GROUP * full_turns - 1 - start, start)
        return carry

    lax.fori_loop(0, cells, shift_cell, 0, unroll=8)


def unpack_kernel(got_hbm, head, tail, count, heads_v, heads_s, store, got, sem):
    copy = pltpu.make_async_copy(got_hbm, got, sem)
    copy.start()
    copy.wait()
    peers = got.shape[0] // PEER_ROWS
    pairs = store.shape[0] - 1
    heads = jnp.transpose(got[pl.ds(FIELDS, peers, stride=PEER_ROWS), :])
    heads_v[0:2, :] = heads[0:2].astype(jnp.int32)
    heads_v[2:4, :] = heads[SLOTS : SLOTS + 2].astype(jnp.int32)
    copy = pltpu.make_async_copy(heads_v, heads_s, sem)
    copy.start()
    copy.wait()
    half_of = lane_iota((FIELDS, 128)) // SLOTS

    def take(source, carry):
        tile = got[pl.ds(source * PEER_ROWS, FIELDS), :]
        turned = pltpu.roll(tile, SLOTS, 1)
        for half in range(2):
            slot = heads_s[2 * half, source]
            slot = jnp.where(slot < 0, 2 * pairs, slot)
            count[slot] = heads_s[2 * half + 1, source]
            side = lax.rem(slot, 2)
            value = jnp.where(side == half, tile, turned)
            pltpu.store(store.at[slot // 2], value, mask=half_of == side)
        return carry

    lax.fori_loop(0, peers, take, 0, unroll=32)
    head[...] = store[0 : pairs // 2]
    tail[...] = store[pairs // 2 : pairs]


def two_halves(tile, low):
    turned = pltpu.roll(tile, SLOTS, 1)
    return (tile, turned), low


def put_halves(tile, low, first, second, index):
    turned = pltpu.roll(tile, SLOTS, 1)
    zero = jnp.zeros_like(tile)
    first[index] = jnp.where(low, tile, zero).astype(first.dtype)
    second[index] = jnp.where(low, zero, turned).astype(first.dtype)
    first[index + 1] = jnp.where(low, turned, zero).astype(first.dtype)
    second[index + 1] = jnp.where(low, zero, tile).astype(first.dtype)


def lane_sums(picks, value):
    total = jnp.zeros((FIELDS, value.shape[0]), F32)
    for part in split_bf16(value, 2):
        total = total + lax.dot_general(
            picks, part.astype(BF16), (((1,), (1,)), ((), ())), preferred_element_type=F32
        )
    return total


def over_items(lists, cells, one_cell, acc, sums, picks):
    fulls, halves, starts = lists
    full_turns = starts[cells]
    quads = GROUP // QUAD

    def add_up(step):
        for n in range(quads):
            sums[step * quads + n] = lane_sums(picks, acc[step * quads + n])

    def turns(chosen, each, skipped):
        def turn(step, carry):
            add_up(jnp.maximum(skipped + step - 1, 0))
            place = (skipped + step) * GROUP
            values = []
            for local in range(GROUP // each):
                cell = chosen[step * (GROUP // each) + local]
                values += one_cell(cell, place + each * local, local, each)
            for n, value in enumerate(values):
                acc[(skipped + step) * quads + n // QUAD, n % QUAD * CHUNK : n % QUAD * CHUNK + CHUNK, :] = value
            return carry

        return turn

    lax.fori_loop(0, full_turns, turns(fulls, 2, 0), 0)
    lax.fori_loop(0, starts[cells + 1], turns(halves, 1, full_turns), 0)
    add_up(full_turns + starts[cells + 1] - 1)


def pair_sums(sums, starts, pair, group):
    total = None
    for n in range(4):
        place = starts[2 * pair + n // 2] + n % 2
        tile = pltpu.roll(sums[place // QUAD], ((n - place) & 3) * CHUNK, 1)
        total = tile if total is None else jnp.where(group == n, tile, total)
    return total


def entries(adj, cell, dummy):
    return [adj[n, cell] for n in range(NEIGH)] + [dummy]


def density_kernel(
    fulls, halves, starts, adj, left, head, tail, right, h, dens, coef_head, coef_tail,
    terms_a, terms_b, ext, stage, lhs, own_r, rows_t, rows_f, acc, sums, raw,
):
    rim = 2 * head.shape[0]
    quarter = head.shape[0]
    dummy = 4 * rim
    low8 = lane_iota((FIELDS, 128)) < SLOTS
    low32 = lane_iota((TERMS, 128)) < SLOTS
    sub8 = sub_iota((FIELDS, 128))

    if True:
        ext[dummy] = jnp.where(sub8 == 7, 1.0, 0.0)
        terms_a[dummy] = jnp.zeros((TERMS, 128), BF16)
        terms_b[dummy] = jnp.zeros((TERMS, 128), BF16)
        ones = jnp.where(sub8 < 3, 1.0, 0.0)
        for part, ref in enumerate((left, head, tail, right)):
            for pair in range(quarter):
                tile = ref[pair]
                slot = part * rim + 2 * pair
                turned = pltpu.roll(tile, SLOTS, 1)
                ext[slot] = jnp.where(low8, tile, turned)
                ext[slot + 1] = jnp.where(low8, turned, tile)
                x, y, z = tile[0:1], tile[1:2], tile[2:3]
                length = x * x + y * y + z * z
                vector = jnp.where(sub8 == 3, -length, tile)
                v1, v2, v3 = split_bf16(vector, 3)
                at = slot // 2 % 8
                for row, v in enumerate((v1, v2, v3, v1, v2, v1)):
                    stage[at, 4 * row : 4 * row + 4, :] = v[0:4]
                stage[at, 24:32, :] = ones
                put_halves(stage[at], low32, terms_a, terms_b, slot)
                if part in (1, 2):
                    own = (part - 1) * quarter + pair
                    vector = jnp.where(sub8 == 3, 1.0, 2.0 * tile)
                    w1, w2, w3 = split_bf16(vector, 3)
                    a1, a2, a3 = split_bf16(1.0 - length, 3)
                    at = 8 + pair % 8
                    for row, w in enumerate((w1, w1, w1, w2, w2, w3)):
                        stage[at, 4 * row : 4 * row + 4, :] = w[0:4]
                    extra = jnp.where(sub8 == 0, a1, jnp.where(sub8 == 1, a2, a3))
                    stage[at, 24:32, :] = jnp.where(sub8 < 3, extra, tile[7:8])
                    turned = jnp.transpose(stage[at])
                    radius = jnp.broadcast_to(turned[:, 31:32], (128, 128))
                    lhs[2 * own : 2 * own + 2] = turned.astype(BF16).reshape(2, SLOTS, TERMS)
                    own_r[2 * own : 2 * own + 2] = radius.reshape(2, SLOTS, 128)

    item_lane = lane_iota((CHUNK, 128))
    item_sub = sub_iota((CHUNK, 128))

    def one_cell(cell, place, at, each):
        index = entries(adj, cell, dummy)
        for p in range(ROWS):
            i, j = index[2 * p], index[2 * p + 1]
            rows_f[at, p] = jnp.where(low8, ext[i], ext[j])
            rows_t[at, :, p * 128 : p * 128 + 128] = terms_a[i] + terms_b[j]
        own = lhs[cell, 0 : each * CHUNK]
        totals = [jnp.zeros((CHUNK, 128), F32) for _ in range(each)]
        for p2 in range(ROWS // 2):
            wide = jnp.dot(
                own, rows_t[at, :, p2 * 256 : p2 * 256 + 256], preferred_element_type=F32
            )
            for p in (2 * p2, 2 * p2 + 1):
                for part in range(each):
                    first = part * CHUNK
                    q = wide[first : first + CHUNK, (p % 2) * 128 : (p % 2) * 128 + 128]
                    q = jnp.maximum(q, 0.0)
                    q2 = q * q
                    totals[part] = totals[part] + q2 * (q * rows_f[at, p, 6:7, :])
                    ri = own_r[cell, first : first + CHUNK]
                    value = q2 * pl.reciprocal(ri + rows_f[at, p, 7:8, :])
                    if p == 0:
                        value = jnp.where(item_lane == item_sub + first, 0.0, value)
                    h[place + part, p] = value
        return totals

    over_items((fulls, halves, starts), 4 * quarter, one_cell, acc, sums, jnp.ones((FIELDS, 128), BF16))

    if True:
        group = lane_iota((FIELDS, 128)) // CHUNK
        for pair in range(2 * quarter):
            total = pair_sums(sums, starts, pair, group)
            raw[pair : pair + 1, :] = total[0:1]
        for part, (ref, coef) in enumerate(((head, coef_head), (tail, coef_tail))):
            mass = ref[:, 6, :]
            live = mass > 0.0
            value = dens_scale * raw[part * quarter : (part + 1) * quarter, :]
            dens[part * quarter : (part + 1) * quarter, :] = jnp.where(live, value, 0.0)
            coef[...] = (2.0 * visc_scale) * mass / jnp.where(live, value, 1.0)


def sweep_kernel(is_first, fulls, halves, starts, adj, h, *refs):
    coefs, speeds, refs = refs[:4], refs[4:8], refs[8:]
    if is_first:
        (head, tail), (out_head, out_tail, below), refs = speeds[1:3], refs[:3], refs[3:]
    else:
        (head, tail, below), (out,), refs = refs[:3], refs[3:4], refs[4:]
    ext, rows, acc, sums = refs
    quarter = head.shape[0]
    rim = 2 * quarter
    dummy = 4 * rim
    lane = lane_iota((FIELDS, 128))
    low = lane < SLOTS
    sub = sub_iota((FIELDS, 128))
    moving = (sub >= 3) & (sub < 6)
    ext[dummy] = jnp.zeros((FIELDS, 128), F32)
    for part in range(4):
        for pair in range(quarter):
            tile = jnp.where(sub == 2, 1.0, jnp.where(moving, speeds[part][pair], 0.0))
            tile = tile * coefs[part][pair : pair + 1, :]
            turned = pltpu.roll(tile, SLOTS, 1)
            slot = part * rim + 2 * pair
            ext[slot] = jnp.where(low, tile, turned)
            ext[slot + 1] = jnp.where(low, turned, tile)
    order = (3, 5, 4, 2)
    item_group = lane_iota((CHUNK, 128)) // CHUNK
    item_low = item_group < 2
    item_even = item_group % 2 == 0

    def merge(a, b):
        if b is None:
            return a + pltpu.roll(a, 64, 1)
        return jnp.where(item_low, a, b) + pltpu.roll(jnp.where(item_low, b, a), 64, 1)

    def one_cell(cell, place, at, each):
        index = entries(adj, cell, dummy)
        for p in range(ROWS):
            rows[at, p] = jnp.where(low, ext[index[2 * p]], ext[index[2 * p + 1]])
        merged = []
        for part in range(each):
            totals = [jnp.zeros((CHUNK, 128), F32) for _ in order]
            for p in range(ROWS):
                value = h[place + part, p]
                for n, f in enumerate(order):
                    if is_first or f != 2:
                        totals[n] = totals[n] + value * rows[at, p, f : f + 1, :]
            even = merge(totals[0], totals[2])
            odd = merge(totals[1], totals[3] if is_first else None)
            other = jnp.where(item_even, odd, even)
            moved = jnp.where(item_even, pltpu.roll(other, 96, 1), pltpu.roll(other, 32, 1))
            merged.append(jnp.where(item_even, even, odd) + moved)
        return merged

    group = lane // CHUNK
    picks = jnp.zeros((FIELDS, 128), jnp.bool_)
    for n, f in enumerate(order):
        picks = picks | ((group == n) & (sub == f))
    picks = picks.astype(F32).astype(BF16)
    over_items((fulls, halves, starts), 2 * rim, one_cell, acc, sums, picks)
    for part, ref in enumerate((head, tail)):
        for pair in range(quarter):
            slot = part * quarter + pair
            tile = ref[pair]
            total = pair_sums(sums, starts, slot, group)
            if is_first:
                weight = total[2:3]
                below[slot : slot + 1, :] = weight
            else:
                weight = below[slot : slot + 1, :]
            live = jnp.broadcast_to(tile[6:7] > 0.0, (FIELDS, 128))
            rate = mass_rate * tile[6:7]
            under = jnp.broadcast_to(rate + weight, (FIELDS, 128))
            value = (rate * tile + total) / jnp.where(live, under, 1.0)
            value = jnp.where(live & moving, value, 0.0)
            if is_first:
                (out_head, out_tail)[part][pair] = value
            else:
                out[:, slot * 128 : slot * 128 + 128] = value[3:6]


def call(kernel, outs, scratch, in_specs, args, out_specs, grid=(), scalars=0, vmem=40):
    return pl.pallas_call(
        kernel,
        out_shape=outs,
        grid_spec=pltpu.PrefetchScalarGridSpec(
            num_scalar_prefetch=scalars,
            grid=grid,
            in_specs=in_specs,
            out_specs=out_specs,
            scratch_shapes=scratch,
        ),
        compiler_params=pltpu.CompilerParams(vmem_limit_bytes=vmem * MIB),
    )(*args)


def on_chip(values):
    return tuple(pltpu.with_memory_space_constraint(v, VMEM) for v in values)


def f32(*shape):
    return jax.ShapeDtypeStruct(shape, F32)


def spec(space):
    return pl.BlockSpec(memory_space=space)


def whole(*shape):
    return pl.BlockSpec(shape, lambda *scalars: (0,) * len(shape))


def density(lists, adj, left, head, tail, right):
    quarter = head.shape[0]
    cells, pairs = 4 * quarter, 2 * quarter
    ext = 2 * cells + 1
    tile = whole(quarter, FIELDS, 128)
    block = spec(VMEM)
    return call(
        density_kernel,
        [pltpu.VMEM((2 * cells + GROUP, ROWS, CHUNK, 128), F32)]
        + [f32(pairs, 128), f32(quarter, 128), f32(quarter, 128)],
        [pltpu.VMEM((ext, TERMS, 128), BF16)] * 2
        + [
            pltpu.VMEM((ext, FIELDS, 128), F32),
            pltpu.VMEM((16, TERMS, 128), F32),
            pltpu.VMEM((cells, SLOTS, TERMS), BF16),
            pltpu.VMEM((cells, SLOTS, 128), F32),
            pltpu.VMEM((GROUP, TERMS, WIDTH), BF16),
            pltpu.VMEM((GROUP, ROWS, FIELDS, 128), F32),
            pltpu.VMEM(((2 * cells + GROUP) // QUAD, 128, 128), F32),
            pltpu.VMEM(((2 * cells + GROUP) // QUAD + 1, FIELDS, 128), F32),
            pltpu.VMEM((pairs, 128), F32),
        ],
        [spec(VMEM)] * 4,
        (*lists, adj, *on_chip((left, head, tail, right))),
        out_specs=[block] + [whole(pairs, 128), whole(quarter, 128), whole(quarter, 128)],
        vmem=22,
        scalars=4,
    )


def sweep(is_first, lists, adj, h, coefs, speeds, own):
    quarter = speeds[0].shape[0]
    cells, pairs = 4 * quarter, 2 * quarter
    ext = 2 * cells + 1
    tile = whole(quarter, FIELDS, 128)
    own_specs = [tile, tile, whole(pairs, 128)][: len(own)]
    if is_first:
        outs = [f32(quarter, FIELDS, 128)] * 2 + [f32(pairs, 128)]
        out_specs = [tile] * 2 + [whole(pairs, 128)]
    else:
        outs, out_specs = [f32(3, cells * SLOTS)], [whole(3, cells * SLOTS)]
    return call(
        functools.partial(sweep_kernel, is_first),
        outs,
        [
            pltpu.VMEM((ext, FIELDS, 128), F32),
            pltpu.VMEM((GROUP, ROWS, FIELDS, 128), F32),
            pltpu.VMEM(((2 * cells + GROUP) // QUAD, 128, 128), F32),
            pltpu.VMEM(((2 * cells + GROUP) // QUAD + 1, FIELDS, 128), F32),
        ],
        [spec(VMEM)] * (9 + len(own)),
        (*lists, adj, h) + tuple(coefs) + tuple(speeds) + own,
        out_specs=out_specs,
        vmem=22,
        scalars=4,
    )


def body(pos, speed, force, weight, heat, share, tally, peer, place, adj):
    peers = lax.axis_size("cells")
    rank = lax.axis_index("cells")
    cells = tally.shape[0]
    rim = cells // 2
    quarter = cells // 4
    pairs = cells // 2
    right_going = [(i, i + 1) for i in range(peers - 1)]
    left_going = [(i + 1, i) for i in range(peers - 1)]

    def rims(head, tail):
        return lax.ppermute(tail, "cells", right_going), lax.ppermute(head, "cells", left_going)

    args = (tally, peer, place, pos, speed, force)
    args = args + tuple(v.reshape(pairs, 128) for v in (weight, heat, share))
    args = tuple(pltpu.with_memory_space_constraint(v, HBM) for v in args)
    (sent,) = call(
        pack_kernel,
        [pltpu.HBM((peers * PEER_ROWS, 128), F32)],
        [(pltpu.SMEM if i < 3 else pltpu.VMEM)(v.shape, v.dtype) for i, v in enumerate(args)]
        + [
            pltpu.VMEM((peers * PEER_ROWS, 128), F32),
            pltpu.VMEM((pairs, FIELDS, 128), F32),
            pltpu.SMEM((peers,), jnp.int32),
            pltpu.SemaphoreType.DMA((9,)),
            pltpu.SemaphoreType.DMA,
        ],
        [spec(HBM)] * 9,
        args,
        out_specs=[spec(HBM)],
    )
    got = lax.all_to_all(
        sent.reshape(peers, 1, PEER_ROWS * 128), "cells", split_axis=0, concat_axis=0, tiled=True
    )
    head, tail, count = call(
        unpack_kernel,
        [f32(quarter, FIELDS, 128)] * 2
        + [jax.ShapeDtypeStruct((cells + 1,), jnp.int32)],
        [
            pltpu.VMEM((4, 128), jnp.int32),
            pltpu.SMEM((4, 128), jnp.int32),
            pltpu.VMEM((pairs + 1, FIELDS, 128), F32),
            pltpu.VMEM((peers * PEER_ROWS, 128), F32),
            pltpu.SemaphoreType.DMA,
        ],
        [spec(HBM)],
        (got.reshape(peers * PEER_ROWS, 128),),
        out_specs=[spec(VMEM)] * 2 + [spec(SMEM)],
    )
    left, right = rims(head, tail)
    lists = call(
        list_kernel,
        [jax.ShapeDtypeStruct((n,), jnp.int32) for n in (cells + GROUP, cells + GROUP, cells + 2)],
        [],
        [spec(SMEM)],
        (count,),
        out_specs=[spec(SMEM)] * 3,
    )
    local = adj - (rank * cells - rim).astype(jnp.int32)
    adj = jnp.concatenate([local[13:14], local[:13], local[14:]], axis=0)
    h, dens, coef_head, coef_tail = density(lists, adj, left, head, tail, right)
    h = pltpu.with_memory_space_constraint(h, VMEM)
    coef_left, coef_right = rims(coef_head, coef_tail)
    coefs = (coef_left, coef_head, coef_tail, coef_right)
    first_head, first_tail, below = sweep(
        True, lists, adj, h, coefs, (left, head, tail, right), ()
    )
    first_left, first_right = rims(first_head, first_tail)
    speeds = (first_left, first_head, first_tail, first_right)
    (out,) = sweep(False, lists, adj, h, coefs, speeds, (head, tail, below))
    return out, dens.reshape(cells * SLOTS)


def solution(mesh):
    split, per_column = P("cells"), P(None, "cells")
    return jax.shard_map(
        body,
        mesh=mesh,
        in_specs=(per_column,) * 3 + (split,) * 6 + (per_column,),
        out_specs=(per_column, split),
        check_vma=False,
    )
```

```python
import functools

import jax
import jax.numpy as jnp
from jax import lax
from jax.experimental import pallas as pl
from jax.experimental.pallas import tpu as pltpu
from jax.sharding import PartitionSpec as P

SLOTS = 64
NEIGH = 27
ENTRY_ORDER = (13,) + tuple(range(13)) + tuple(range(14, 27))
ROWS = 14
WIDTH = ROWS * 128
CHUNK = 32
GROUP = 8
QUAD = 4
FIELDS = 8
PEER_ROWS = FIELDS + 1
TERMS = 32

step_time = 0.5
mass_rate = 0.3
visc_scale = 0.01
dens_scale = 0.01
heat_slope = 3.0
jamming_bound = 0.6

VMEM = pltpu.MemorySpace.VMEM
SMEM = pltpu.MemorySpace.SMEM
HBM = pltpu.MemorySpace.HBM
MIB = 1 << 20
BF16 = jnp.bfloat16
F32 = jnp.float32


def lane_iota(shape):
    return lax.broadcasted_iota(jnp.int32, shape, len(shape) - 1)


def sub_iota(shape):
    return lax.broadcasted_iota(jnp.int32, shape, len(shape) - 2)


def split_bf16(value, count):
    parts = []
    for _ in range(count):
        part = value.astype(BF16).astype(F32)
        parts.append(part)
        value = value - part
    return parts


def pack_kernel(*refs):
    inputs, sent, local, out, fields, seen, sems, out_sem = refs[:9], refs[9], refs[10:19], *refs[19:]
    copies = [pltpu.make_async_copy(a, b, sems.at[i]) for i, (a, b) in enumerate(zip(inputs, local))]
    for copy in copies:
        copy.start()
    tally, peer, place, pos, speed, force, weight, heat, share = local
    cells = tally.shape[0]
    peers = out.shape[0] // PEER_ROWS
    lane = lane_iota((1, 128))
    low = lane < SLOTS

    def clear(index, carry):
        seen[index] = 0
        out[pl.ds(index * PEER_ROWS + FIELDS, 1), :] = jnp.full((1, 128), -1.0, F32)
        return carry

    lax.fori_loop(0, peers, clear, 0, unroll=32)
    for copy in copies:
        copy.wait()
    open_bound = 1.0 - share[...] / jamming_bound
    resist = jnp.exp(heat_slope * heat[...]) * (open_bound * open_bound * jnp.sqrt(open_bound))
    for pair in range(cells // 2):
        span = pl.ds(pair * 128, 128)
        bound = jnp.where(low, tally[2 * pair], tally[2 * pair + 1] + SLOTS)
        live = (lane < bound).astype(F32)
        fields[pair, 0:3, :] = pos[:, span]
        fields[pair, 3:6, :] = speed[:, span] + step_time * force[:, span]
        fields[pair, 6:7, :] = weight[pair : pair + 1, :] * live
        fields[pair, 7:8, :] = resist[pair : pair + 1, :]
    half_of = lane_iota((FIELDS, 128)) // SLOTS

    def send(pair, carry):
        tile = fields[pair]
        turned = pltpu.roll(tile, SLOTS, 1)
        for side in range(2):
            cell = 2 * pair + side
            target = peer[cell]
            half = seen[target]
            seen[target] = 1
            row = target * PEER_ROWS
            value = jnp.where(half == side, tile, turned)
            pltpu.store(out.at[pl.ds(row, FIELDS), :], value, mask=half_of == half)
            first = half * SLOTS
            head = jnp.where(lane == first, place[cell].astype(F32), tally[cell].astype(F32))
            pltpu.store(
                out.at[pl.ds(row + FIELDS, 1), :], head, mask=(lane == first) | (lane == first + 1)
            )
        return carry

    lax.fori_loop(0, cells // 2, send, 0, unroll=20)
    copy = pltpu.make_async_copy(out, sent, out_sem)
    copy.start()
    copy.wait()


def list_kernel(count, fulls, halves, starts):
    cells = starts.shape[0] - 2
    for index in range(fulls.shape[0]):
        fulls[index] = 0
    for index in range(halves.shape[0]):
        halves[index] = 0

    def list_cell(cell, carry):
        full, half = carry
        fulls[full] = cell
        halves[half] = cell
        more = (count[cell] > CHUNK).astype(jnp.int32)
        starts[cell] = jnp.where(more > 0, 2 * full, -1 - half)
        return full + more, half + 1 - more

    full, half = lax.fori_loop(0, cells, list_cell, (0, 0), unroll=8)
    full_turns = (2 * full + GROUP - 1) // GROUP
    starts[cells] = full_turns
    starts[cells + 1] = (half + GROUP - 1) // GROUP

    def shift_cell(cell, carry):
        start = starts[cell]
        starts[cell] = jnp.where(start < 0, GROUP * full_turns - 1 - start, start)
        return carry

    lax.fori_loop(0, cells, shift_cell, 0, unroll=8)


def unpack_kernel(got_hbm, head, tail, count, heads_v, heads_s, store, got, sem):
    copy = pltpu.make_async_copy(got_hbm, got, sem)
    copy.start()
    copy.wait()
    peers = got.shape[0] // PEER_ROWS
    pairs = store.shape[0] - 1
    heads = jnp.transpose(got[pl.ds(FIELDS, peers, stride=PEER_ROWS), :])
    heads_v[0:2, :] = heads[0:2].astype(jnp.int32)
    heads_v[2:4, :] = heads[SLOTS : SLOTS + 2].astype(jnp.int32)
    copy = pltpu.make_async_copy(heads_v, heads_s, sem)
    copy.start()
    copy.wait()
    half_of = lane_iota((FIELDS, 128)) // SLOTS

    def take(source, carry):
        tile = got[pl.ds(source * PEER_ROWS, FIELDS), :]
        turned = pltpu.roll(tile, SLOTS, 1)
        for half in range(2):
            slot = heads_s[2 * half, source]
            slot = jnp.where(slot < 0, 2 * pairs, slot)
            count[slot] = heads_s[2 * half + 1, source]
            side = lax.rem(slot, 2)
            value = jnp.where(side == half, tile, turned)
            pltpu.store(store.at[slot // 2], value, mask=half_of == side)
        return carry

    lax.fori_loop(0, peers, take, 0, unroll=64)
    head[...] = store[0 : pairs // 2]
    tail[...] = store[pairs // 2 : pairs]


def two_halves(tile, low):
    turned = pltpu.roll(tile, SLOTS, 1)
    return (tile, turned), low


def put_halves(tile, low, first, second, index):
    turned = pltpu.roll(tile, SLOTS, 1)
    zero = jnp.zeros_like(tile)
    first[index] = jnp.where(low, tile, zero).astype(first.dtype)
    second[index] = jnp.where(low, zero, turned).astype(first.dtype)
    first[index + 1] = jnp.where(low, turned, zero).astype(first.dtype)
    second[index + 1] = jnp.where(low, zero, tile).astype(first.dtype)


def lane_sums(picks, value):
    total = jnp.zeros((FIELDS, value.shape[0]), F32)
    for part in split_bf16(value, 2):
        total = total + lax.dot_general(
            picks, part.astype(BF16), (((1,), (1,)), ((), ())), preferred_element_type=F32
        )
    return total


def over_items(lists, cells, one_cell, acc, sums, picks):
    fulls, halves, starts = lists
    full_turns = starts[cells]
    quads = GROUP // QUAD

    def add_up(step):
        for n in range(quads):
            sums[step * quads + n] = lane_sums(picks, acc[step * quads + n])

    def turns(chosen, each, skipped):
        def turn(step, carry):
            add_up(jnp.maximum(skipped + step - 1, 0))
            place = (skipped + step) * GROUP
            values = []
            for local in range(GROUP // each):
                cell = chosen[step * (GROUP // each) + local]
                values += one_cell(cell, place + each * local, local, each)
            for n, value in enumerate(values):
                acc[(skipped + step) * quads + n // QUAD, n % QUAD * CHUNK : n % QUAD * CHUNK + CHUNK, :] = value
            return carry

        return turn

    lax.fori_loop(0, full_turns, turns(fulls, 2, 0), 0)
    lax.fori_loop(0, starts[cells + 1], turns(halves, 1, full_turns), 0)
    add_up(full_turns + starts[cells + 1] - 1)


def pair_sums(sums, starts, pair, group):
    total = None
    for n in range(4):
        place = starts[2 * pair + n // 2] + n % 2
        tile = pltpu.roll(sums[place // QUAD], ((n - place) & 3) * CHUNK, 1)
        total = tile if total is None else jnp.where(group == n, tile, total)
    return total


def entries(adj, cell, dummy):
    return [adj[n, cell] for n in range(NEIGH)] + [dummy]


def density_kernel(
    fulls, halves, starts, adj, left, head, tail, right, h, dens, coef_head, coef_tail,
    terms_a, terms_b, ext, stage, lhs, own_r, rows_t, rows_f, acc, sums, raw,
):
    rim = 2 * head.shape[0]
    quarter = head.shape[0]
    dummy = 4 * rim
    low8 = lane_iota((FIELDS, 128)) < SLOTS
    low32 = lane_iota((TERMS, 128)) < SLOTS
    sub8 = sub_iota((FIELDS, 128))

    if True:
        ext[dummy] = jnp.where(sub8 == 7, 1.0, 0.0)
        terms_a[dummy] = jnp.zeros((TERMS, 128), BF16)
        terms_b[dummy] = jnp.zeros((TERMS, 128), BF16)
        ones = jnp.where(sub8 < 3, 1.0, 0.0)
        for part, ref in enumerate((left, head, tail, right)):
            for pair in range(quarter):
                tile = ref[pair]
                slot = part * rim + 2 * pair
                turned = pltpu.roll(tile, SLOTS, 1)
                ext[slot] = jnp.where(low8, tile, turned)
                ext[slot + 1] = jnp.where(low8, turned, tile)
                x, y, z = tile[0:1], tile[1:2], tile[2:3]
                length = x * x + y * y + z * z
                vector = jnp.where(sub8 == 3, -length, tile)
                v1, v2, v3 = split_bf16(vector, 3)
                at = slot // 2 % 8
                for row, v in enumerate((v1, v2, v3, v1, v2, v1)):
                    stage[at, 4 * row : 4 * row + 4, :] = v[0:4]
                stage[at, 24:32, :] = ones
                put_halves(stage[at], low32, terms_a, terms_b, slot)
                if part in (1, 2):
                    own = (part - 1) * quarter + pair
                    vector = jnp.where(sub8 == 3, 1.0, 2.0 * tile)
                    w1, w2, w3 = split_bf16(vector, 3)
                    a1, a2, a3 = split_bf16(1.0 - length, 3)
                    at = 8 + pair % 8
                    for row, w in enumerate((w1, w1, w1, w2, w2, w3)):
                        stage[at, 4 * row : 4 * row + 4, :] = w[0:4]
                    extra = jnp.where(sub8 == 0, a1, jnp.where(sub8 == 1, a2, a3))
                    stage[at, 24:32, :] = jnp.where(sub8 < 3, extra, tile[7:8])
                    turned = jnp.transpose(stage[at])
                    radius = jnp.broadcast_to(turned[:, 31:32], (128, 128))
                    lhs[2 * own : 2 * own + 2] = turned.astype(BF16).reshape(2, SLOTS, TERMS)
                    own_r[2 * own : 2 * own + 2] = radius.reshape(2, SLOTS, 128)

    item_lane = lane_iota((CHUNK, 128))
    item_sub = sub_iota((CHUNK, 128))

    def one_cell(cell, place, at, each):
        index = entries(adj, cell, dummy)
        for p in range(ROWS):
            i, j = index[2 * p], index[2 * p + 1]
            rows_f[at, p] = jnp.where(low8, ext[i], ext[j])
            rows_t[at, :, p * 128 : p * 128 + 128] = terms_a[i] + terms_b[j]
        own = lhs[cell, 0 : each * CHUNK]
        totals = [jnp.zeros((CHUNK, 128), F32) for _ in range(each)]
        for p2 in range(ROWS // 2):
            wide = jnp.dot(
                own, rows_t[at, :, p2 * 256 : p2 * 256 + 256], preferred_element_type=F32
            )
            for p in (2 * p2, 2 * p2 + 1):
                for part in range(each):
                    first = part * CHUNK
                    q = wide[first : first + CHUNK, (p % 2) * 128 : (p % 2) * 128 + 128]
                    q = jnp.maximum(q, 0.0)
                    q2 = q * q
                    totals[part] = totals[part] + q2 * (q * rows_f[at, p, 6:7, :])
                    ri = own_r[cell, first : first + CHUNK]
                    value = q2 * pl.reciprocal(ri + rows_f[at, p, 7:8, :])
                    if p == 0:
                        value = jnp.where(item_lane == item_sub + first, 0.0, value)
                    h[place + part, p] = value
        return totals

    over_items((fulls, halves, starts), 4 * quarter, one_cell, acc, sums, jnp.ones((FIELDS, 128), BF16))

    if True:
        group = lane_iota((FIELDS, 128)) // CHUNK
        for pair in range(2 * quarter):
            total = pair_sums(sums, starts, pair, group)
            raw[pair : pair + 1, :] = total[0:1]
        for part, (ref, coef) in enumerate(((head, coef_head), (tail, coef_tail))):
            mass = ref[:, 6, :]
            live = mass > 0.0
            value = dens_scale * raw[part * quarter : (part + 1) * quarter, :]
            dens[part * quarter : (part + 1) * quarter, :] = jnp.where(live, value, 0.0)
            coef[...] = (2.0 * visc_scale) * mass / jnp.where(live, value, 1.0)


def sweep_kernel(is_first, fulls, halves, starts, adj, h, *refs):
    coefs, speeds, refs = refs[:4], refs[4:8], refs[8:]
    if is_first:
        (head, tail), (out_head, out_tail, below), refs = speeds[1:3], refs[:3], refs[3:]
    else:
        (head, tail, below), (out,), refs = refs[:3], refs[3:4], refs[4:]
    ext, rows, acc, sums = refs
    quarter = head.shape[0]
    rim = 2 * quarter
    dummy = 4 * rim
    lane = lane_iota((FIELDS, 128))
    low = lane < SLOTS
    sub = sub_iota((FIELDS, 128))
    moving = (sub >= 3) & (sub < 6)
    ext[dummy] = jnp.zeros((FIELDS, 128), F32)
    for part in range(4):
        for pair in range(quarter):
            tile = jnp.where(sub == 2, 1.0, jnp.where(moving, speeds[part][pair], 0.0))
            tile = tile * coefs[part][pair : pair + 1, :]
            turned = pltpu.roll(tile, SLOTS, 1)
            slot = part * rim + 2 * pair
            ext[slot] = jnp.where(low, tile, turned)
            ext[slot + 1] = jnp.where(low, turned, tile)
    order = (3, 5, 4, 2)
    item_group = lane_iota((CHUNK, 128)) // CHUNK
    item_low = item_group < 2
    item_even = item_group % 2 == 0

    def merge(a, b):
        if b is None:
            return a + pltpu.roll(a, 64, 1)
        return jnp.where(item_low, a, b) + pltpu.roll(jnp.where(item_low, b, a), 64, 1)

    def one_cell(cell, place, at, each):
        index = entries(adj, cell, dummy)
        for p in range(ROWS):
            rows[at, p] = jnp.where(low, ext[index[2 * p]], ext[index[2 * p + 1]])
        merged = []
        for part in range(each):
            totals = [jnp.zeros((CHUNK, 128), F32) for _ in order]
            for p in range(ROWS):
                value = h[place + part, p]
                for n, f in enumerate(order):
                    if is_first or f != 2:
                        totals[n] = totals[n] + value * rows[at, p, f : f + 1, :]
            even = merge(totals[0], totals[2])
            odd = merge(totals[1], totals[3] if is_first else None)
            other = jnp.where(item_even, odd, even)
            moved = jnp.where(item_even, pltpu.roll(other, 96, 1), pltpu.roll(other, 32, 1))
            merged.append(jnp.where(item_even, even, odd) + moved)
        return merged

    group = lane // CHUNK
    picks = jnp.zeros((FIELDS, 128), jnp.bool_)
    for n, f in enumerate(order):
        picks = picks | ((group == n) & (sub == f))
    picks = picks.astype(F32).astype(BF16)
    over_items((fulls, halves, starts), 2 * rim, one_cell, acc, sums, picks)
    for part, ref in enumerate((head, tail)):
        for pair in range(quarter):
            slot = part * quarter + pair
            tile = ref[pair]
            total = pair_sums(sums, starts, slot, group)
            if is_first:
                weight = total[2:3]
                below[slot : slot + 1, :] = weight
            else:
                weight = below[slot : slot + 1, :]
            live = jnp.broadcast_to(tile[6:7] > 0.0, (FIELDS, 128))
            rate = mass_rate * tile[6:7]
            under = jnp.broadcast_to(rate + weight, (FIELDS, 128))
            value = (rate * tile + total) / jnp.where(live, under, 1.0)
            value = jnp.where(live & moving, value, 0.0)
            if is_first:
                (out_head, out_tail)[part][pair] = value
            else:
                out[:, slot * 128 : slot * 128 + 128] = value[3:6]


def call(kernel, outs, scratch, in_specs, args, out_specs, grid=(), scalars=0, vmem=40):
    return pl.pallas_call(
        kernel,
        out_shape=outs,
        grid_spec=pltpu.PrefetchScalarGridSpec(
            num_scalar_prefetch=scalars,
            grid=grid,
            in_specs=in_specs,
            out_specs=out_specs,
            scratch_shapes=scratch,
        ),
        compiler_params=pltpu.CompilerParams(vmem_limit_bytes=vmem * MIB),
    )(*args)


def on_chip(values):
    return tuple(pltpu.with_memory_space_constraint(v, VMEM) for v in values)


def f32(*shape):
    return jax.ShapeDtypeStruct(shape, F32)


def spec(space):
    return pl.BlockSpec(memory_space=space)


def whole(*shape):
    return pl.BlockSpec(shape, lambda *scalars: (0,) * len(shape))


def density(lists, adj, left, head, tail, right):
    quarter = head.shape[0]
    cells, pairs = 4 * quarter, 2 * quarter
    ext = 2 * cells + 1
    tile = whole(quarter, FIELDS, 128)
    block = spec(VMEM)
    return call(
        density_kernel,
        [pltpu.VMEM((2 * cells + GROUP, ROWS, CHUNK, 128), F32)]
        + [f32(pairs, 128), f32(quarter, 128), f32(quarter, 128)],
        [pltpu.VMEM((ext, TERMS, 128), BF16)] * 2
        + [
            pltpu.VMEM((ext, FIELDS, 128), F32),
            pltpu.VMEM((16, TERMS, 128), F32),
            pltpu.VMEM((cells, SLOTS, TERMS), BF16),
            pltpu.VMEM((cells, SLOTS, 128), F32),
            pltpu.VMEM((GROUP, TERMS, WIDTH), BF16),
            pltpu.VMEM((GROUP, ROWS, FIELDS, 128), F32),
            pltpu.VMEM(((2 * cells + GROUP) // QUAD, 128, 128), F32),
            pltpu.VMEM(((2 * cells + GROUP) // QUAD + 1, FIELDS, 128), F32),
            pltpu.VMEM((pairs, 128), F32),
        ],
        [spec(VMEM)] * 4,
        (*lists, adj, *on_chip((left, head, tail, right))),
        out_specs=[block] + [whole(pairs, 128), whole(quarter, 128), whole(quarter, 128)],
        vmem=22,
        scalars=4,
    )


def sweep(is_first, lists, adj, h, coefs, speeds, own):
    quarter = speeds[0].shape[0]
    cells, pairs = 4 * quarter, 2 * quarter
    ext = 2 * cells + 1
    tile = whole(quarter, FIELDS, 128)
    own_specs = [tile, tile, whole(pairs, 128)][: len(own)]
    if is_first:
        outs = [f32(quarter, FIELDS, 128)] * 2 + [f32(pairs, 128)]
        out_specs = [tile] * 2 + [whole(pairs, 128)]
    else:
        outs, out_specs = [f32(3, cells * SLOTS)], [whole(3, cells * SLOTS)]
    return call(
        functools.partial(sweep_kernel, is_first),
        outs,
        [
            pltpu.VMEM((ext, FIELDS, 128), F32),
            pltpu.VMEM((GROUP, ROWS, FIELDS, 128), F32),
            pltpu.VMEM(((2 * cells + GROUP) // QUAD, 128, 128), F32),
            pltpu.VMEM(((2 * cells + GROUP) // QUAD + 1, FIELDS, 128), F32),
        ],
        [spec(VMEM)] * (9 + len(own)),
        (*lists, adj, h) + tuple(coefs) + tuple(speeds) + own,
        out_specs=out_specs,
        vmem=22,
        scalars=4,
    )


def body(pos, speed, force, weight, heat, share, tally, peer, place, adj):
    peers = lax.axis_size("cells")
    rank = lax.axis_index("cells")
    cells = tally.shape[0]
    rim = cells // 2
    quarter = cells // 4
    pairs = cells // 2
    right_going = [(i, i + 1) for i in range(peers - 1)]
    left_going = [(i + 1, i) for i in range(peers - 1)]

    def rims(head, tail):
        return lax.ppermute(tail, "cells", right_going), lax.ppermute(head, "cells", left_going)

    args = (tally, peer, place, pos, speed, force)
    args = args + tuple(v.reshape(pairs, 128) for v in (weight, heat, share))
    args = tuple(pltpu.with_memory_space_constraint(v, HBM) for v in args)
    (sent,) = call(
        pack_kernel,
        [pltpu.HBM((peers * PEER_ROWS, 128), F32)],
        [(pltpu.SMEM if i < 3 else pltpu.VMEM)(v.shape, v.dtype) for i, v in enumerate(args)]
        + [
            pltpu.VMEM((peers * PEER_ROWS, 128), F32),
            pltpu.VMEM((pairs, FIELDS, 128), F32),
            pltpu.SMEM((peers,), jnp.int32),
            pltpu.SemaphoreType.DMA((9,)),
            pltpu.SemaphoreType.DMA,
        ],
        [spec(HBM)] * 9,
        args,
        out_specs=[spec(HBM)],
    )
    got = lax.all_to_all(
        sent.reshape(peers, 1, PEER_ROWS * 128), "cells", split_axis=0, concat_axis=0, tiled=True
    )
    head, tail, count = call(
        unpack_kernel,
        [f32(quarter, FIELDS, 128)] * 2
        + [jax.ShapeDtypeStruct((cells + 1,), jnp.int32)],
        [
            pltpu.VMEM((4, 128), jnp.int32),
            pltpu.SMEM((4, 128), jnp.int32),
            pltpu.VMEM((pairs + 1, FIELDS, 128), F32),
            pltpu.VMEM((peers * PEER_ROWS, 128), F32),
            pltpu.SemaphoreType.DMA,
        ],
        [spec(HBM)],
        (got.reshape(peers * PEER_ROWS, 128),),
        out_specs=[spec(VMEM)] * 2 + [spec(SMEM)],
    )
    left, right = rims(head, tail)
    lists = call(
        list_kernel,
        [jax.ShapeDtypeStruct((n,), jnp.int32) for n in (cells + GROUP, cells + GROUP, cells + 2)],
        [],
        [spec(SMEM)],
        (count,),
        out_specs=[spec(SMEM)] * 3,
    )
    local = adj - (rank * cells - rim).astype(jnp.int32)
    adj = jnp.concatenate([local[13:14], local[:13], local[14:]], axis=0)
    h, dens, coef_head, coef_tail = density(lists, adj, left, head, tail, right)
    h = pltpu.with_memory_space_constraint(h, VMEM)
    coef_left, coef_right = rims(coef_head, coef_tail)
    coefs = (coef_left, coef_head, coef_tail, coef_right)
    first_head, first_tail, below = sweep(
        True, lists, adj, h, coefs, (left, head, tail, right), ()
    )
    first_left, first_right = rims(first_head, first_tail)
    speeds = (first_left, first_head, first_tail, first_right)
    (out,) = sweep(False, lists, adj, h, coefs, speeds, (head, tail, below))
    return out, dens.reshape(cells * SLOTS)


def solution(mesh):
    split, per_column = P("cells"), P(None, "cells")
    return jax.shard_map(
        body,
        mesh=mesh,
        in_specs=(per_column,) * 3 + (split,) * 6 + (per_column,),
        out_specs=(per_column, split),
        check_vma=False,
    )
```
